32 devices in a mesh: rep: 2 (over y), ep: 8 (over z, x), tp: 2 (over core).
Axes of the slice: x: 2, y: 2, z: 4, core: 2. Of those that a mesh axis runs over, the one named last changes fastest.
Arguments:
- resid: bfloat16 [1024, 1440], P(('rep', 'ep')), parts along dimension 0, may hold values from -6 to 6
- query: bfloat16 [1024, 2048], P(('rep', 'ep'), 'tp'), parts along dimension 0, may hold values from -400 to 400
- key_value_pages: bfloat16 [2, 12288, 16, 256], P(None, ('rep', 'ep'), None, 'tp'), parts along dimension 1, may hold values from -4 to 4
- page_table: int32 [1024, 12], P(('rep', 'ep')), parts along dimension 0, may hold values from 0 to 767, as said below
- ctx_len: int32 [1024], P(('rep', 'ep')), parts along dimension 0, may hold values from 2 to 192, as said below
- experts_chosen: int32 [1024, 4], P(('rep', 'ep')), parts along dimension 0, may hold values from 0 to 7, as said below
- router_logits: float32 [1024, 4], P(('rep', 'ep')), parts along dimension 0, may hold values from -25 to 300
- norm_gain: float32 [1440], replicated, may hold values from 0.25 to 1.75
- out_proj: bfloat16 [2048, 1440], P('tp'), may hold values from -0.125 to 0.125
- w_gate: bfloat16 [8, 1440, 1440], P('ep', None, 'tp'), may hold values from -0.15625 to 0.15625
- w_up: bfloat16 [8, 1440, 1440], P('ep', None, 'tp'), may hold values from -0.15625 to 0.15625
- w_down: bfloat16 [8, 1440, 1440], P('ep', 'tp'), may hold values from -3 to 3
Outputs:
- mixed: bfloat16 [1024, 1440], P(('rep', 'ep'), 'tp'), parts along dimension 0
The draws below stay inside these ranges and needn't reach their ends.
There are 2 independent parts, one for each index of `rep`. The reference program is written for one: setup_inputs(seed, part) draws one part's arguments, and reference() takes and returns one part's arrays. A program takes and returns all parts, laid end to end along the dimension named above; an argument that names none is the same for every part. Nothing has to cross between parts.
Inputs may be any that keep to these rules, and one draw needn't show every extreme that they name: Each block of 64 tokens holds its own pool: the rows of page_table of one block together name each of its 768 pages once. `ctx_len`: every block of 64 tokens has a token with 192 positions. `experts_chosen`: each row names 4 different experts. Within the rows of one device no expert is named by more than 64 rows, and one expert is named by exactly 64 of them.
All inputs are finite; a program needn't handle non-finite values.
Results may differ from the reference program's by a relative error of at most 0.008.
Values may be sent and summed in bfloat16 or wider, within the bound.
No kernel may reach another device: no remote copies, remote signals or barrier semaphores. Data moves between devices by JAX's collectives and lax.ppermute only.
A program may use at most 128 MiB of HBM per device.

```python
import math
import jax
import jax.numpy as jnp
from jax import lax

D = 1440
QUERY_HEADS = 32
KEY_VALUE_HEADS = 4
HEAD_WIDTH = 64
FF = 1440
TOP = 4
PAGE_LENGTH = 16
CONTEXT_LIMIT = 192
TOKENS_PER_SHARD = 64
E = 8
TOKEN_COUNT = 512
CAP = 64
PAGES_TOK = 12
PAGES_PER_SHARD = 768


def table_draw(key):
    blocks = TOKEN_COUNT // TOKENS_PER_SHARD
    subkeys = jax.random.split(jax.random.fold_in(key, 101), blocks)

    def one_pool(subkey):
        return jax.random.permutation(subkey, PAGES_PER_SHARD)
    orders = jax.vmap(one_pool)(subkeys)
    return orders.reshape(TOKEN_COUNT, PAGES_TOK).astype(jnp.int32)


def route_draw(key):
    blocks = TOKEN_COUNT // TOKENS_PER_SHARD
    pairs = TOKENS_PER_SHARD * TOP
    slot_total = E * CAP

    def one_block(subkey):
        parts = jax.random.split(subkey, 5)
        hottest = jax.random.randint(parts[0], (), 0, E, jnp.int32)
        owner = jnp.arange(slot_total, dtype=jnp.int32) // CAP
        favour = jax.random.randint(parts[1], (E,), 0, 3, jnp.int32)
        jitter = jax.random.randint(parts[2], (slot_total,), 0, 65536, jnp.int32)
        priority = jitter + favour[owner] * 32768 + jnp.where(owner == hottest, 1048576, 0).astype(jnp.int32)
        priority = priority * slot_total + jnp.arange(slot_total, dtype=jnp.int32)
        taken = lax.top_k(priority, pairs)[1].astype(jnp.int32)
        ordered = jnp.sort(taken)
        names = (ordered // CAP).reshape(TOP, TOKENS_PER_SHARD).T
        names = names[jax.random.permutation(parts[3], TOKENS_PER_SHARD)]
        column_rank = jax.random.randint(parts[4], (TOKENS_PER_SHARD, TOP), 0, 65536, jnp.int32) * TOP + jnp.arange(TOP, dtype=jnp.int32)[None, :]
        column_order = jnp.argsort(column_rank, axis=1)
        return jnp.take_along_axis(names, column_order, axis=1).astype(jnp.int32)
    subkeys = jax.random.split(jax.random.fold_in(key, 201), blocks)
    return jax.vmap(one_block)(subkeys).reshape(TOKEN_COUNT, TOP).astype(jnp.int32)


def cache_base(key):
    target_shape = (2, TOKEN_COUNT // TOKENS_PER_SHARD * PAGES_PER_SHARD, PAGE_LENGTH, KEY_VALUE_HEADS * HEAD_WIDTH)
    return jax.random.truncated_normal(jax.random.fold_in(key, 104), -4.0, 4.0, target_shape, jnp.float32)


def draw_resid(key, part):
    values = jax.random.truncated_normal(jax.random.fold_in(key, 401), -6.0, 6.0, (TOKEN_COUNT, D), jnp.float32)
    return values.astype(jnp.bfloat16)


def draw_page_table(key, part):
    return table_draw(key)


def draw_ctx_len(key, part):
    blocks = TOKEN_COUNT // TOKENS_PER_SHARD
    lengths = jax.random.randint(jax.random.fold_in(key, 102), (TOKEN_COUNT,), 2, CONTEXT_LIMIT + 1, jnp.int32)
    chosen_row = jax.random.randint(jax.random.fold_in(key, 103), (blocks,), 0, TOKENS_PER_SHARD, jnp.int32)
    marked = jnp.arange(TOKEN_COUNT, dtype=jnp.int32) % TOKENS_PER_SHARD == jnp.repeat(chosen_row, TOKENS_PER_SHARD)
    return jnp.where(marked, CONTEXT_LIMIT, lengths).astype(jnp.int32)


def draw_experts_chosen(key, part):
    return route_draw(key)


def draw_key_value_pages(key, part):
    cache_pages = cache_base(key)
    return cache_pages.astype(jnp.bfloat16)


def draw_query(key, part):
    values = jax.random.truncated_normal(jax.random.fold_in(key, 107), -4.0, 4.0, (TOKEN_COUNT, QUERY_HEADS * HEAD_WIDTH), jnp.float32)
    return values.astype(jnp.bfloat16)


def draw_router_logits(key, part):
    values = jnp.clip(2.0 * jax.random.normal(jax.random.fold_in(key, 109), (TOKEN_COUNT, TOP), jnp.float32), -10.0, 10.0)
    return values


def draw_w_down(key, part):
    values = jax.random.truncated_normal(jax.random.fold_in(key, 301), -4.0, 4.0, (E, FF, D), jnp.float32) / math.sqrt(FF)
    return values.astype(jnp.bfloat16)


def block_scale(own_key, dims, shards, smallest, largest):
    factor_of, own = 1.0, jax.random.fold_in(own_key, 6)
    for position, shards_of in shards:
        heights = jnp.exp(jax.random.uniform(jax.random.fold_in(own, position), (shards_of,), jnp.float32, smallest / len(shards), largest / len(shards)))
        factor_of = factor_of * jnp.repeat(heights, dims[position] // shards_of).reshape([-1 if axis == position else 1 for axis in range(len(dims))])
    return factor_of


def noise(rng, dims, width, reach, cuts=(), kind=jnp.bfloat16):
    drawn = width * jax.random.normal(rng, dims, jnp.float32)
    if cuts:
        drawn = drawn * block_scale(rng, dims, cuts, -0.22, 0.18)
    return jnp.clip(drawn, -reach, reach).astype(kind)


def setup_inputs(seed: int = 0, part: int = 0) -> dict:
    key_of = jax.random.split(jax.random.key(seed), 13)
    own_keys = jax.random.split(jax.random.fold_in(key_of[12], part), 13)
    return {
        "resid": draw_resid(jax.random.fold_in(jax.random.fold_in(key_of[12], part), 71), part),
        "query": draw_query(jax.random.fold_in(jax.random.fold_in(key_of[12], part), 71), part),
        "key_value_pages": draw_key_value_pages(jax.random.fold_in(jax.random.fold_in(key_of[12], part), 71), part),
        "page_table": draw_page_table(jax.random.fold_in(jax.random.fold_in(key_of[12], part), 71), part),
        "ctx_len": draw_ctx_len(jax.random.fold_in(jax.random.fold_in(key_of[12], part), 71), part),
        "experts_chosen": draw_experts_chosen(jax.random.fold_in(jax.random.fold_in(key_of[12], part), 71), part),
        "router_logits": draw_router_logits(jax.random.fold_in(jax.random.fold_in(key_of[12], part), 71), part),
        "norm_gain": jnp.clip(1.0 + 0.15 * jax.random.normal(key_of[7], (D,), jnp.float32), 0.25, 1.75),
        "out_proj": noise(key_of[8], (QUERY_HEADS * HEAD_WIDTH, D), (QUERY_HEADS * HEAD_WIDTH) ** -0.5, 0.125, ((0, 2),)),
        "w_gate": noise(key_of[9], (E, D, FF), D ** -0.5, 0.15625, ((0, 8), (2, 2))),
        "w_up": noise(key_of[10], (E, D, FF), D ** -0.5, 0.15625, ((0, 8), (2, 2))),
        "w_down": draw_w_down(jax.random.fold_in(key_of[12], 71), part),
    }


def reference(resid, query, key_value_pages, page_table, ctx_len, experts_chosen, router_logits, norm_gain, out_proj, w_gate, w_up, w_down):
    blocks = TOKEN_COUNT // TOKENS_PER_SHARD
    group_width = QUERY_HEADS // KEY_VALUE_HEADS

    def attend(index):
        start = index * TOKENS_PER_SHARD
        query_matrix = lax.dynamic_slice_in_dim(query, start, TOKENS_PER_SHARD, 0)
        page_table_rows = lax.dynamic_slice_in_dim(page_table, start, TOKENS_PER_SHARD, 0) + index * PAGES_PER_SHARD
        lengths = lax.dynamic_slice_in_dim(ctx_len, start, TOKENS_PER_SHARD, 0)
        cached_keys = key_value_pages[0][page_table_rows].reshape(TOKENS_PER_SHARD, CONTEXT_LIMIT, KEY_VALUE_HEADS, HEAD_WIDTH).astype(jnp.float32)
        cached_values = key_value_pages[1][page_table_rows].reshape(TOKENS_PER_SHARD, CONTEXT_LIMIT, KEY_VALUE_HEADS, HEAD_WIDTH).astype(jnp.float32)
        query_block = query_matrix.reshape(TOKENS_PER_SHARD, KEY_VALUE_HEADS, group_width, HEAD_WIDTH).astype(jnp.float32)
        scores = jnp.einsum('tgqd,tpgd->tgqp', query_block, cached_keys) * (1.0 / math.sqrt(HEAD_WIDTH))
        visible = jnp.arange(CONTEXT_LIMIT, dtype=jnp.int32)[None, :] < lengths[:, None]
        scores = jnp.where(visible[:, None, None, :], scores, -jnp.inf)
        row_max = lax.optimization_barrier(jnp.max(scores, axis=3, keepdims=True))
        weights = jnp.exp(scores - row_max)
        probability = (weights / lax.optimization_barrier(jnp.sum(weights, axis=3, keepdims=True))).astype(jnp.bfloat16)
        attended = jnp.einsum('tgqp,tpgd->tgqd', probability.astype(jnp.float32), cached_values)
        return attended.astype(jnp.bfloat16).reshape(TOKENS_PER_SHARD, QUERY_HEADS * HEAD_WIDTH)
    attended = lax.map(attend, jnp.arange(blocks, dtype=jnp.int32)).reshape(TOKEN_COUNT, QUERY_HEADS * HEAD_WIDTH)
    stream = resid.astype(jnp.float32) + jnp.dot(attended, out_proj, preferred_element_type=jnp.float32)
    mean_square = lax.optimization_barrier(jnp.mean(stream * stream, axis=1, keepdims=True))
    normed = (stream * lax.rsqrt(mean_square + 1e-05) * norm_gain).astype(jnp.bfloat16)
    gate_weights = jax.nn.softmax(router_logits.astype(jnp.float32), axis=1)
    chosen = experts_chosen.reshape(blocks, TOKENS_PER_SHARD * TOP)
    onehot = (chosen[:, :, None] == jnp.arange(E, dtype=jnp.int32)[None, None, :]).astype(jnp.int32)
    before = jnp.cumsum(onehot, axis=1, dtype=jnp.int32) - onehot
    slot_rank = lax.optimization_barrier(jnp.sum(before * onehot, axis=2, dtype=jnp.int32)).reshape(-1)
    chosen_flat = chosen.reshape(-1)
    source = jnp.repeat(jnp.arange(blocks, dtype=jnp.int32), TOKENS_PER_SHARD * TOP)
    token_rows = jnp.repeat(jnp.arange(TOKEN_COUNT, dtype=jnp.int32), TOP)
    buffer = jnp.zeros((E, blocks, CAP, D), jnp.bfloat16)
    buffer = buffer.at[chosen_flat, source, slot_rank].set(normed[token_rows])

    def expert_apply(operands):
        inputs, gate_matrix, up_matrix, down_matrix = operands
        rows = inputs.reshape(blocks * CAP, D)
        gate_value = jnp.dot(rows, gate_matrix, preferred_element_type=jnp.float32)
        up_value = jnp.dot(rows, up_matrix, preferred_element_type=jnp.float32)
        hidden = (gate_value * jax.nn.sigmoid(1.702 * gate_value) * (up_value + 1.0)).astype(jnp.bfloat16)
        output = jnp.dot(hidden, down_matrix, preferred_element_type=jnp.float32).astype(jnp.bfloat16)
        return output.reshape(blocks, CAP, D)
    outputs = lax.map(expert_apply, (buffer, w_gate, w_up, w_down))
    picked = outputs[chosen_flat, source, slot_rank].astype(jnp.float32).reshape(TOKEN_COUNT, TOP, D)
    expert_mix = lax.optimization_barrier(jnp.sum(picked * gate_weights[:, :, None], axis=1))
    return (stream + expert_mix).astype(jnp.bfloat16)
```

```python
import functools
import math

import jax
import jax.numpy as jnp
from jax import lax
from jax.experimental import pallas as pl
from jax.experimental.pallas import tpu as pltpu
from jax.sharding import PartitionSpec as P

HEAD_WIDTH = 64
LANES = 128

SMEM = pl.BlockSpec(memory_space=pltpu.SMEM)
VMEM = pl.BlockSpec(memory_space=pltpu.VMEM)
ANY = pl.BlockSpec(memory_space=pl.ANY)


def attend_kernel(
    heads, unroll, table, length, q_ref, pages, proj, out_wide, out_sent, kbuf, vbuf, wbuf, qs, os, sem
):
    tokens = q_ref.shape[0]
    per_token = table.shape[0]
    lanes = kbuf.shape[2]
    positions = per_token * kbuf.shape[1]
    copies = [
        pltpu.make_async_copy(pages.at[0], kbuf, sem.at[0]),
        pltpu.make_async_copy(pages.at[1], vbuf, sem.at[1]),
        pltpu.make_async_copy(proj, wbuf, sem.at[2]),
    ]
    for copy in copies:
        copy.start()
    low = lax.broadcasted_iota(jnp.int32, (tokens, lanes), 1) < HEAD_WIDTH
    half = heads // 2
    for h in range(heads):
        pair = q_ref[:, (h // 2) * lanes : (h // 2 + 1) * lanes].astype(jnp.float32)
        if (h < half) != (h % 2 == 0):
            pair = pltpu.roll(pair, HEAD_WIDTH, 1)
        row = jnp.where(low if h < half else ~low, pair, 0.0)
        qs[pl.ds(h, tokens, stride=heads), :] = row * (1.0 / math.sqrt(HEAD_WIDTH))
    copies[0].wait()
    copies[1].wait()
    spot = lax.broadcasted_iota(jnp.int32, (heads, positions), 1)

    @pl.loop(0, tokens // unroll)
    def _(step):
        scores, values = [], []
        for u in range(unroll):
            t = step * unroll + u
            ids = [table[i, t] for i in range(per_token)]
            keys = jnp.concatenate([kbuf[i] for i in ids], axis=0)
            values.append(jnp.concatenate([vbuf[i] for i in ids], axis=0))
            q = qs[pl.ds(pl.multiple_of(t * heads, heads), heads), :].astype(jnp.bfloat16)
            s = lax.dot_general(
                q, keys, (((1,), (1,)), ((), ())), preferred_element_type=jnp.float32
            )
            scores.append(jnp.where(spot < length[t], s, -jnp.inf))
        s = jnp.concatenate(scores, axis=0)
        w = jnp.exp(s - jnp.max(s, axis=1, keepdims=True))
        total = jnp.sum(w, axis=1, keepdims=True)
        p = w.astype(jnp.bfloat16)
        o = jnp.concatenate(
            [
                jnp.dot(p[u * heads : (u + 1) * heads], values[u], preferred_element_type=jnp.float32)
                for u in range(unroll)
            ],
            axis=0,
        )
        rows = unroll * heads
        os[pl.ds(pl.multiple_of(step * rows, rows), rows), :] = o / total

    parts = []
    for j in range(half):
        even = os[pl.ds(2 * j, tokens, stride=heads), :]
        odd = os[pl.ds(2 * j + 1, tokens, stride=heads), :]
        if 2 * j < half:
            odd = pltpu.roll(odd, HEAD_WIDTH, 1)
        else:
            even = pltpu.roll(even, HEAD_WIDTH, 1)
        parts.append(jnp.where(low, even, odd).astype(jnp.bfloat16))
    attended = jnp.concatenate(parts, axis=1)
    copies[2].wait()
    part = lax.dot_general(
        attended, wbuf[...], (((1,), (1,)), ((), ())), preferred_element_type=jnp.float32
    )
    out_wide[...] = part
    out_sent[...] = part.astype(jnp.bfloat16)


def attend(query, pages, page_table, ctx_len, out_proj):
    tokens = query.shape[0]
    heads = query.shape[1] // HEAD_WIDTH
    width = out_proj.shape[1]
    lanes = pages.shape[3]
    rows = (tokens * heads, lanes)
    return pl.pallas_call(
        functools.partial(attend_kernel, heads, min(16, tokens)),
        out_shape=(
            jax.ShapeDtypeStruct((tokens, width), jnp.float32),
            jax.ShapeDtypeStruct((tokens, width), jnp.bfloat16),
        ),
        in_specs=[SMEM, SMEM, VMEM, ANY, ANY],
        out_specs=(VMEM, VMEM),
        scratch_shapes=[
            pltpu.VMEM(pages.shape[1:], pages.dtype),
            pltpu.VMEM(pages.shape[1:], pages.dtype),
            pltpu.VMEM(out_proj.shape[::-1], out_proj.dtype),
            pltpu.VMEM(rows, jnp.float32),
            pltpu.VMEM(rows, jnp.float32),
            pltpu.SemaphoreType.DMA((3,)),
        ],
        name="attend",
    )(page_table.T, ctx_len, query, pages, out_proj.T)


def norm_kernel(experts, resid, own, other, gain, chosen, logits, stream_out, all_out, mine_out):
    tokens, width = own.shape
    side = lax.axis_index("tp")
    half_cols = stream_out.shape[1]
    stream = resid[...].astype(jnp.float32) + own[...] + other[...].astype(jnp.float32)
    mean_square = jnp.sum(stream * stream, axis=1, keepdims=True) / width
    normed = stream * lax.rsqrt(mean_square + 1e-05) * gain[...]
    left, right = stream[:, :half_cols], stream[:, half_cols:]
    stream_out[...] = jnp.where(side == 0, left, right)
    all_out[:, :width] = normed.astype(jnp.bfloat16)
    logit = logits[...]
    gate = jnp.exp(logit - jnp.max(logit, axis=1, keepdims=True))
    gate = gate / jnp.sum(gate, axis=1, keepdims=True)
    spare = all_out.shape[1] - width
    column = lax.broadcasted_iota(jnp.int32, (tokens, spare), 1)
    name = jnp.where(column < experts, column, column - experts)
    dense = jnp.zeros((tokens, spare), jnp.float32)
    for k in range(chosen.shape[1]):
        dense += jnp.where(chosen[:, k : k + 1] == name, gate[:, k : k + 1], 0.0)
    coarse = dense.astype(jnp.bfloat16).astype(jnp.float32)
    fine = jnp.where(column < 2 * experts, dense - coarse, 0.0)
    all_out[:, width:] = jnp.where(column < experts, coarse, fine).astype(jnp.bfloat16)
    rows = tokens // 2
    mine_out[...] = all_out[pl.ds(pl.multiple_of(side * rows, rows), rows), :]


def norm(resid, own, other, gain, chosen, logits, experts, padded):
    tokens, width = own.shape
    return pl.pallas_call(
        functools.partial(norm_kernel, experts),
        out_shape=(
            jax.ShapeDtypeStruct((tokens, width // 2), jnp.float32),
            jax.ShapeDtypeStruct((tokens, padded), jnp.bfloat16),
            jax.ShapeDtypeStruct((tokens // 2, padded), jnp.bfloat16),
        ),
        in_specs=[VMEM] * 6,
        out_specs=(VMEM,) * 3,
        name="norm",
    )(resid, own, other, gain[None], chosen, logits)


def expert_kernel(experts, blocks, *refs):
    halves = refs[: 2 * blocks]
    w_gate, w_up, w_down, keep_out, send_out, xs = refs[2 * blocks :]
    side = lax.axis_index("tp")
    me = lax.axis_index("ep")
    width = w_gate.shape[0]
    rows = halves[0].shape[0]
    for b in range(blocks):
        here = pl.multiple_of(b * 2 * rows + side * rows, rows)
        there = pl.multiple_of(b * 2 * rows + (1 - side) * rows, rows)
        xs[pl.ds(here, rows), :] = halves[2 * b][...]
        xs[pl.ds(there, rows), :] = halves[2 * b + 1][...]
    x = xs[:, :width]
    spare = xs[:, width:].astype(jnp.float32)
    column = lax.broadcasted_iota(jnp.int32, spare.shape, 1)
    mine = (column == me) | (column == me + experts)
    gate = jnp.sum(jnp.where(mine, spare, 0.0), axis=1, keepdims=True)
    g = jnp.dot(x, w_gate[...], preferred_element_type=jnp.float32)
    u = jnp.dot(x, w_up[...], preferred_element_type=jnp.float32)
    hidden = (g * jax.nn.sigmoid(1.702 * g) * (u + 1.0)).astype(jnp.bfloat16)
    y = jnp.dot(hidden, w_down[...], preferred_element_type=jnp.float32) * gate
    half_cols = keep_out.shape[1]
    left, right = y[:, :half_cols], y[:, half_cols:]
    keep_out[...] = jnp.where(side == 0, left, right)
    send_out[...] = jnp.where(side == 0, right, left).astype(jnp.bfloat16)


def expert(halves, w_gate, w_up, w_down, experts):
    blocks = len(halves) // 2
    half_rows, padded = halves[0].shape
    rows = blocks * 2 * half_rows
    width = w_down.shape[1]
    return pl.pallas_call(
        functools.partial(expert_kernel, experts, blocks),
        out_shape=(
            jax.ShapeDtypeStruct((rows, width // 2), jnp.float32),
            jax.ShapeDtypeStruct((rows, width // 2), jnp.bfloat16),
        ),
        in_specs=[VMEM] * (2 * blocks + 3),
        out_specs=(VMEM,) * 2,
        scratch_shapes=[pltpu.VMEM((rows, padded), jnp.bfloat16)],
        name="expert",
    )(*halves, w_gate, w_up, w_down)


def flip(value, axis, offset):
    return lax.ppermute(value, axis, [(i, i ^ offset) for i in range(lax.axis_size(axis))])


def routed_all(stream, whole, mine, w_gate, w_up, w_down, experts):
    owners = lax.axis_size("ep")
    tokens = whole.shape[0]
    half_rows = tokens // 2
    side = lax.axis_index("tp")
    halves = []
    for k in range(1, owners):
        near = flip(mine, "ep", k)
        halves += [near, flip(near, "tp", 1)]
    other = lax.dynamic_slice_in_dim(whole, (1 - side) * half_rows, half_rows, 0)
    halves += [mine, other]
    keep, send = expert(halves, w_gate[0], w_up[0], w_down[0], experts)
    full = keep + flip(send, "tp", 1).astype(jnp.float32)
    mixed = stream + full[(owners - 1) * tokens :]
    for k in range(1, owners):
        part = full[(k - 1) * tokens : k * tokens].astype(jnp.bfloat16)
        mixed = mixed + flip(part, "ep", k).astype(jnp.float32)
    return mixed.astype(jnp.bfloat16)


def routed_slots(stream, normed, experts_chosen, router_logits, w_gate, w_up, w_down, capacity):
    tok_rows, top_count = experts_chosen.shape
    local_experts = w_gate.shape[0]
    owners = lax.axis_size("ep")
    experts = local_experts * owners
    gate_weights = jax.nn.softmax(router_logits, axis=1)
    chosen_flat = experts_chosen.reshape(-1)
    onehot = (chosen_flat[:, None] == jnp.arange(experts, dtype=jnp.int32)[None, :]).astype(
        jnp.int32
    )
    before = jnp.cumsum(onehot, axis=0, dtype=jnp.int32) - onehot
    slot_rank = jnp.sum(before * onehot, axis=1, dtype=jnp.int32)
    slot_index = (chosen_flat * capacity + slot_rank).reshape(tok_rows, top_count)
    slot_range = jnp.arange(experts * capacity, dtype=jnp.int32)
    placed = slot_index[:, :, None] == slot_range[None, None, :]
    dispatch = jnp.sum(placed.astype(jnp.float32), axis=1).astype(jnp.bfloat16)
    outgoing = lax.dot_general(
        dispatch, normed, (((0,), (0,)), ((), ())), preferred_element_type=jnp.float32
    )
    outgoing = outgoing.astype(jnp.bfloat16).reshape(
        owners, local_experts, capacity, normed.shape[1]
    )
    arrived_full = lax.all_gather(
        lax.all_to_all(outgoing, "ep", split_axis=0, concat_axis=0, tiled=True),
        "tp",
        axis=3,
        tiled=True,
    )
    gate_value = jnp.einsum(
        "sekd,edf->sekf", arrived_full, w_gate, preferred_element_type=jnp.float32
    )
    up_value = jnp.einsum("sekd,edf->sekf", arrived_full, w_up, preferred_element_type=jnp.float32)
    hidden = (gate_value * jax.nn.sigmoid(1.702 * gate_value) * (up_value + 1.0)).astype(
        jnp.bfloat16
    )
    partial_value = jnp.einsum("sekf,efd->sekd", hidden, w_down, preferred_element_type=jnp.float32)
    finished = lax.psum_scatter(partial_value, "tp", scatter_dimension=3, tiled=True).astype(
        jnp.bfloat16
    )
    returned = lax.all_to_all(finished, "ep", split_axis=0, concat_axis=0, tiled=True)
    combine = jnp.sum(placed.astype(jnp.float32) * gate_weights[:, :, None], axis=1)
    expert_mix = jnp.dot(
        combine,
        returned.reshape(experts * capacity, -1).astype(jnp.float32),
        precision=lax.Precision.HIGHEST,
    )
    return (stream + expert_mix).astype(jnp.bfloat16)


def body(
    resid,
    query,
    key_value_pages,
    page_table,
    ctx_len,
    experts_chosen,
    router_logits,
    norm_gain,
    out_proj,
    w_gate,
    w_up,
    w_down,
):
    tok_rows, model_width = resid.shape
    top_count = experts_chosen.shape[1]
    local_experts = w_gate.shape[0]
    owners = lax.axis_size("ep")
    experts = local_experts * owners
    capacity = max(2, min(tok_rows, 2 * tok_rows * top_count // experts))
    padded = -(-model_width // LANES) * LANES

    own, sent = attend(query, key_value_pages, page_table, ctx_len, out_proj)
    other = flip(sent, "tp", 1)
    if (
        local_experts == 1
        and tok_rows <= capacity
        and model_width + 2 * experts <= padded
        and owners & (owners - 1) == 0
    ):
        stream, whole, mine = norm(
            resid, own, other, norm_gain, experts_chosen, router_logits, experts, padded
        )
        return routed_all(stream, whole, mine, w_gate, w_up, w_down, experts)
    half_cols = model_width // lax.axis_size("tp")
    offset = lax.axis_index("tp") * half_cols
    stream = resid.astype(jnp.float32) + own + other.astype(jnp.float32)
    mean_square = jnp.mean(stream * stream, axis=1, keepdims=True)
    normed = (stream * lax.rsqrt(mean_square + 1e-05) * norm_gain).astype(jnp.bfloat16)
    stream = lax.dynamic_slice_in_dim(stream, offset, half_cols, 1)
    normed = lax.dynamic_slice_in_dim(normed, offset, half_cols, 1)
    return routed_slots(
        stream, normed, experts_chosen, router_logits, w_gate, w_up, w_down, capacity
    )


def solution(mesh):
    return jax.shard_map(
        body,
        mesh=mesh,
        in_specs=(
            P(("rep", "ep"), None),
            P(("rep", "ep"), "tp"),
            P(None, ("rep", "ep"), None, "tp"),
            P(("rep", "ep"), None),
            P(("rep", "ep")),
            P(("rep", "ep"), None),
            P(("rep", "ep"), None),
            P(),
            P("tp", None),
            P("ep", None, "tp"),
            P("ep", None, "tp"),
            P("ep", "tp", None),
        ),
        out_specs=P(("rep", "ep"), "tp"),
        check_vma=False,
    )
```

```python
import functools
import math

import jax
import jax.numpy as jnp
from jax import lax
from jax.experimental import pallas as pl
from jax.experimental.pallas import tpu as pltpu
from jax.sharding import PartitionSpec as P

HEAD_WIDTH = 64
LANES = 128
MIB = 1 << 20

SMEM = pl.BlockSpec(memory_space=pltpu.SMEM)
VMEM = pl.BlockSpec(memory_space=pltpu.VMEM)
HBM = pl.BlockSpec(memory_space=pltpu.HBM)


def dense_gates(experts, chosen, logits, out):
    tokens, columns = out.shape
    gate = jnp.exp(logits[...] - jnp.max(logits[...], axis=0, keepdims=True))
    gate = gate / jnp.sum(gate, axis=0, keepdims=True)
    name = lax.broadcasted_iota(jnp.int32, (columns, tokens), 0)
    fine = name >= experts
    expert = jnp.where(fine, name - experts, name)
    dense = jnp.zeros((columns, tokens), jnp.float32)
    for k in range(chosen.shape[0]):
        dense += jnp.where(chosen[k : k + 1, :] == expert, gate[k : k + 1, :], 0.0)
    coarse = dense.astype(jnp.bfloat16).astype(jnp.float32)
    both = jnp.where(fine, dense - coarse, coarse).astype(jnp.bfloat16)
    row = lax.broadcasted_iota(jnp.int32, (columns, columns), 0)
    unit = (row == lax.broadcasted_iota(jnp.int32, (columns, columns), 1)).astype(jnp.bfloat16)
    turned = lax.dot_general(both, unit, (((0,), (0,)), ((), ())), preferred_element_type=jnp.float32)
    out[...] = turned.astype(jnp.bfloat16)


def attend_kernel(
    heads,
    unroll,
    experts,
    table,
    length,
    q_ref,
    pages,
    proj,
    chosen,
    logits,
    out_wide,
    out_sent,
    out_gates,
    kbuf,
    vbuf,
    wbuf,
    qs,
    os,
    sem,
):
    tokens = q_ref.shape[0]
    per_token = table.shape[0]
    lanes = kbuf.shape[2]
    positions = per_token * kbuf.shape[1]
    copies = [
        pltpu.make_async_copy(pages.at[0], kbuf, sem.at[0]),
        pltpu.make_async_copy(pages.at[1], vbuf, sem.at[1]),
        pltpu.make_async_copy(proj, wbuf, sem.at[2]),
    ]
    for copy in copies:
        copy.start()
    low = lax.broadcasted_iota(jnp.int32, (tokens, lanes), 1) < HEAD_WIDTH
    half = heads // 2
    for h in range(heads):
        pair = q_ref[:, (h // 2) * lanes : (h // 2 + 1) * lanes].astype(jnp.float32)
        if (h < half) != (h % 2 == 0):
            pair = pltpu.roll(pair, HEAD_WIDTH, 1)
        row = jnp.where(low if h < half else ~low, pair, 0.0)
        qs[pl.ds(h, tokens, stride=heads), :] = row * (1.0 / math.sqrt(HEAD_WIDTH))
    dense_gates(experts, chosen, logits, out_gates)
    copies[0].wait()
    copies[1].wait()
    spot = lax.broadcasted_iota(jnp.int32, (heads, positions), 1)

    @pl.loop(0, tokens // unroll)
    def _(step):
        scores, values = [], []
        for u in range(unroll):
            t = step * unroll + u
            ids = [table[i, t] for i in range(per_token)]
            keys = jnp.concatenate([kbuf[i] for i in ids], axis=0)
            values.append(jnp.concatenate([vbuf[i] for i in ids], axis=0))
            q = qs[pl.ds(pl.multiple_of(t * heads, heads), heads), :].astype(jnp.bfloat16)
            s = lax.dot_general(
                q, keys, (((1,), (1,)), ((), ())), preferred_element_type=jnp.float32
            )
            scores.append(jnp.where(spot < length[t], s, -jnp.inf))
        s = jnp.concatenate(scores, axis=0)
        w = jnp.exp(s - jnp.max(s, axis=1, keepdims=True))
        total = jnp.sum(w, axis=1, keepdims=True)
        p = w.astype(jnp.bfloat16)
        o = jnp.concatenate(
            [
                jnp.dot(p[u * heads : (u + 1) * heads], values[u], preferred_element_type=jnp.float32)
                for u in range(unroll)
            ],
            axis=0,
        )
        rows = unroll * heads
        os[pl.ds(pl.multiple_of(step * rows, rows), rows), :] = o / total

    parts = []
    for j in range(half):
        even = os[pl.ds(2 * j, tokens, stride=heads), :]
        odd = os[pl.ds(2 * j + 1, tokens, stride=heads), :]
        if 2 * j < half:
            odd = pltpu.roll(odd, HEAD_WIDTH, 1)
        else:
            even = pltpu.roll(even, HEAD_WIDTH, 1)
        parts.append(jnp.where(low, even, odd).astype(jnp.bfloat16))
    attended = jnp.concatenate(parts, axis=1)
    copies[2].wait()
    part = lax.dot_general(
        attended, wbuf[...], (((1,), (1,)), ((), ())), preferred_element_type=jnp.float32
    )
    out_wide[...] = part
    out_sent[...] = part.astype(jnp.bfloat16)


def attend(query, pages, page_table, ctx_len, out_proj, chosen, logits, experts):
    tokens = query.shape[0]
    heads = query.shape[1] // HEAD_WIDTH
    width = out_proj.shape[1]
    lanes = pages.shape[3]
    rows = (tokens * heads, lanes)
    return pl.pallas_call(
        functools.partial(attend_kernel, heads, min(16, tokens), experts),
        out_shape=(
            jax.ShapeDtypeStruct((tokens, width), jnp.float32),
            jax.ShapeDtypeStruct((tokens, width), jnp.bfloat16),
            jax.ShapeDtypeStruct((tokens, 2 * experts), jnp.bfloat16),
        ),
        in_specs=[SMEM, SMEM, VMEM, HBM, HBM, VMEM, VMEM],
        out_specs=(VMEM,) * 3,
        scratch_shapes=[
            pltpu.VMEM(pages.shape[1:], pages.dtype),
            pltpu.VMEM(pages.shape[1:], pages.dtype),
            pltpu.VMEM(out_proj.shape[::-1], out_proj.dtype),
            pltpu.VMEM(rows, jnp.float32),
            pltpu.VMEM(rows, jnp.float32),
            pltpu.SemaphoreType.DMA((3,)),
        ],
        compiler_params=pltpu.CompilerParams(vmem_limit_bytes=60 * MIB),
        name="attend",
    )(page_table.T, ctx_len, query, pages, out_proj.T, chosen.T, logits.T)


def norm_kernel(resid, own, other, gain, gates, stream_out, all_out, mine_out):
    tokens, width = own.shape
    side = lax.axis_index("tp")
    half_cols = stream_out.shape[1]
    stream = resid[...].astype(jnp.float32) + own[...] + other[...].astype(jnp.float32)
    mean_square = jnp.sum(stream * stream, axis=1, keepdims=True) / width
    normed = stream * lax.rsqrt(mean_square + 1e-05) * gain[...]
    all_out[:, :width] = normed.astype(jnp.bfloat16)
    all_out[:, width : width + gates.shape[1]] = gates[...]
    rows = tokens // 2
    mine_out[...] = all_out[pl.ds(pl.multiple_of(side * rows, rows), rows), :]
    stream_out[...] = jnp.where(side == 0, stream[:, :half_cols], stream[:, half_cols:])


def norm(resid, own, other, gain, gates, padded):
    tokens, width = own.shape
    return pl.pallas_call(
        norm_kernel,
        out_shape=(
            jax.ShapeDtypeStruct((tokens, width // 2), jnp.float32),
            jax.ShapeDtypeStruct((tokens, padded), jnp.bfloat16),
            jax.ShapeDtypeStruct((tokens // 2, padded), jnp.bfloat16),
        ),
        in_specs=[VMEM] * 5,
        out_specs=(VMEM,) * 3,
        compiler_params=pltpu.CompilerParams(vmem_limit_bytes=4 * MIB),
        name="norm",
    )(resid, own, other, gain[None], gates)


def expert_kernel(experts, pieces, *refs):
    sources = refs[:pieces]
    w_gate, w_up, w_down, keep_out, send_out, xs = refs[pieces:]
    side = lax.axis_index("tp")
    me = lax.axis_index("ep")
    width = w_gate.shape[0]
    if pieces == 1:
        xs = sources[0]
    else:
        rows = sources[0].shape[0]
        for b in range(pieces // 2):
            here = pl.multiple_of(b * 2 * rows + side * rows, rows)
            there = pl.multiple_of(b * 2 * rows + (1 - side) * rows, rows)
            xs[pl.ds(here, rows), :] = sources[2 * b][...]
            xs[pl.ds(there, rows), :] = sources[2 * b + 1][...]
    x = xs[:, :width]
    spare = xs[:, width : width + 2 * experts].astype(jnp.float32)
    column = lax.broadcasted_iota(jnp.int32, spare.shape, 1)
    mine = (column == me) | (column == me + experts)
    gate = jnp.sum(jnp.where(mine, spare, 0.0), axis=1, keepdims=True)
    g = jnp.dot(x, w_gate[...], preferred_element_type=jnp.float32)
    u = jnp.dot(x, w_up[...], preferred_element_type=jnp.float32)
    hidden = (g * jax.nn.sigmoid(1.702 * g) * (u + 1.0)).astype(jnp.bfloat16)
    y = jnp.dot(hidden, w_down[...], preferred_element_type=jnp.float32) * gate
    half_cols = y.shape[1] // 2
    left, right = y[:, :half_cols], y[:, half_cols:]
    keep_out[:, :half_cols] = jnp.where(side == 0, left, right)
    send_out[:, :half_cols] = jnp.where(side == 0, right, left).astype(jnp.bfloat16)


def expert(sources, w_gate, w_up, w_down, experts):
    pieces = len(sources)
    rows = sum(s.shape[0] for s in sources)
    padded = sources[0].shape[1]
    out_cols = -(-w_down.shape[1] // 2 // LANES) * LANES
    return pl.pallas_call(
        functools.partial(expert_kernel, experts, pieces),
        out_shape=(
            jax.ShapeDtypeStruct((rows, out_cols), jnp.float32),
            jax.ShapeDtypeStruct((rows, out_cols), jnp.bfloat16),
        ),
        in_specs=[VMEM] * (pieces + 3),
        out_specs=(VMEM,) * 2,
        scratch_shapes=[pltpu.VMEM((rows if pieces > 1 else 16, padded), jnp.bfloat16)],
        compiler_params=pltpu.CompilerParams(vmem_limit_bytes=16 * MIB),
        cost_estimate=pl.CostEstimate(
            flops=6 * rows * w_down.size, transcendentals=0, bytes_accessed=6 * w_down.size
        ),
        name="expert",
    )(*sources, w_gate, w_up, w_down)


def flip(value, axis, offset):
    return lax.ppermute(value, axis, [(i, i ^ offset) for i in range(lax.axis_size(axis))])


def routed_all(stream, whole, mine, w_gate, w_up, w_down, experts):
    owners = lax.axis_size("ep")
    tokens = whole.shape[0]
    bits = [1 << i for i in range(owners.bit_length() - 1)]
    half = {0: mine}
    stages = []
    for count in range(1, len(bits) + 1):
        stages.append([k for k in range(owners) if k.bit_count() == count])
    for stage in stages:
        for k in sorted(stage, reverse=True):
            low = k & -k
            half[k] = flip(half[k - low], "ep", low)
    keep, got = {}, {}

    def work(group, sources):
        kept, sent = expert(sources, w_gate[0], w_up[0], w_down[0], experts)
        received = flip(sent, "tp", 1)
        for i, k in enumerate(group):
            keep[k] = kept[i * tokens : (i + 1) * tokens]
            got[k] = received[i * tokens : (i + 1) * tokens]

    work([0], [whole])
    for stage in stages:
        sources = []
        for k in stage:
            sources += [half[k], flip(half[k], "tp", 1)]
        work(stage, sources)
    total = {k: keep[k] + got[k].astype(jnp.float32) for k in range(owners)}
    for stage in reversed(stages):
        for k in sorted(stage, reverse=True):
            low = k & -k
            part = flip(total[k].astype(jnp.bfloat16), "ep", low)
            total[k - low] = total[k - low] + part.astype(jnp.float32)
    return (stream + total[0][:, : stream.shape[1]]).astype(jnp.bfloat16)


def routed_slots(stream, normed, experts_chosen, router_logits, w_gate, w_up, w_down, capacity):
    tok_rows, top_count = experts_chosen.shape
    local_experts = w_gate.shape[0]
    owners = lax.axis_size("ep")
    experts = local_experts * owners
    gate_weights = jax.nn.softmax(router_logits, axis=1)
    chosen_flat = experts_chosen.reshape(-1)
    onehot = (chosen_flat[:, None] == jnp.arange(experts, dtype=jnp.int32)[None, :]).astype(
        jnp.int32
    )
    before = jnp.cumsum(onehot, axis=0, dtype=jnp.int32) - onehot
    slot_rank = jnp.sum(before * onehot, axis=1, dtype=jnp.int32)
    slot_index = (chosen_flat * capacity + slot_rank).reshape(tok_rows, top_count)
    slot_range = jnp.arange(experts * capacity, dtype=jnp.int32)
    placed = slot_index[:, :, None] == slot_range[None, None, :]
    dispatch = jnp.sum(placed.astype(jnp.float32), axis=1).astype(jnp.bfloat16)
    outgoing = lax.dot_general(
        dispatch, normed, (((0,), (0,)), ((), ())), preferred_element_type=jnp.float32
    )
    outgoing = outgoing.astype(jnp.bfloat16).reshape(
        owners, local_experts, capacity, normed.shape[1]
    )
    arrived_full = lax.all_gather(
        lax.all_to_all(outgoing, "ep", split_axis=0, concat_axis=0, tiled=True),
        "tp",
        axis=3,
        tiled=True,
    )
    gate_value = jnp.einsum(
        "sekd,edf->sekf", arrived_full, w_gate, preferred_element_type=jnp.float32
    )
    up_value = jnp.einsum("sekd,edf->sekf", arrived_full, w_up, preferred_element_type=jnp.float32)
    hidden = (gate_value * jax.nn.sigmoid(1.702 * gate_value) * (up_value + 1.0)).astype(
        jnp.bfloat16
    )
    partial_value = jnp.einsum("sekf,efd->sekd", hidden, w_down, preferred_element_type=jnp.float32)
    finished = lax.psum_scatter(partial_value, "tp", scatter_dimension=3, tiled=True).astype(
        jnp.bfloat16
    )
    returned = lax.all_to_all(finished, "ep", split_axis=0, concat_axis=0, tiled=True)
    combine = jnp.sum(placed.astype(jnp.float32) * gate_weights[:, :, None], axis=1)
    expert_mix = jnp.dot(
        combine,
        returned.reshape(experts * capacity, -1).astype(jnp.float32),
        precision=lax.Precision.HIGHEST,
    )
    return (stream + expert_mix).astype(jnp.bfloat16)


def body(
    resid,
    query,
    key_value_pages,
    page_table,
    ctx_len,
    experts_chosen,
    router_logits,
    norm_gain,
    out_proj,
    w_gate,
    w_up,
    w_down,
):
    tok_rows, model_width = resid.shape
    top_count = experts_chosen.shape[1]
    local_experts = w_gate.shape[0]
    owners = lax.axis_size("ep")
    experts = local_experts * owners
    capacity = max(2, min(tok_rows, 2 * tok_rows * top_count // experts))
    padded = -(-model_width // LANES) * LANES

    own, sent, gates = attend(
        query, key_value_pages, page_table, ctx_len, out_proj, experts_chosen, router_logits, experts
    )
    other = flip(sent, "tp", 1)
    if (
        local_experts == 1
        and tok_rows <= capacity
        and model_width + 2 * experts <= padded
        and owners & (owners - 1) == 0
    ):
        stream, whole, mine = norm(resid, own, other, norm_gain, gates, padded)
        return routed_all(stream, whole, mine, w_gate, w_up, w_down, experts)
    half_cols = model_width // lax.axis_size("tp")
    offset = lax.axis_index("tp") * half_cols
    stream = resid.astype(jnp.float32) + own + other.astype(jnp.float32)
    mean_square = jnp.mean(stream * stream, axis=1, keepdims=True)
    normed = (stream * lax.rsqrt(mean_square + 1e-05) * norm_gain).astype(jnp.bfloat16)
    stream = lax.dynamic_slice_in_dim(stream, offset, half_cols, 1)
    normed = lax.dynamic_slice_in_dim(normed, offset, half_cols, 1)
    return routed_slots(
        stream, normed, experts_chosen, router_logits, w_gate, w_up, w_down, capacity
    )


def solution(mesh):
    return jax.shard_map(
        body,
        mesh=mesh,
        in_specs=(
            P(("rep", "ep"), None),
            P(("rep", "ep"), "tp"),
            P(None, ("rep", "ep"), None, "tp"),
            P(("rep", "ep"), None),
            P(("rep", "ep")),
            P(("rep", "ep"), None),
            P(("rep", "ep"), None),
            P(),
            P("tp", None),
            P("ep", None, "tp"),
            P("ep", None, "tp"),
            P("ep", "tp", None),
        ),
        out_specs=P(("rep", "ep"), "tp"),
        check_vma=False,
    )
```

```python
import functools
import math

import jax
import jax.numpy as jnp
from jax import lax
from jax.experimental import pallas as pl
from jax.experimental.pallas import tpu as pltpu
from jax.sharding import PartitionSpec as P


HEAD_WIDTH = 64
LANES = 128
MIB = 1 << 20

SMEM = pl.BlockSpec(memory_space=pltpu.SMEM)
VMEM = pl.BlockSpec(memory_space=pltpu.VMEM)
HBM = pl.BlockSpec(memory_space=pltpu.HBM)


def dense_gates(experts, chosen, logits, out):
    tokens, columns = out.shape
    gate = jnp.exp(logits[...] - jnp.max(logits[...], axis=0, keepdims=True))
    gate = gate / jnp.sum(gate, axis=0, keepdims=True)
    name = lax.broadcasted_iota(jnp.int32, (columns, tokens), 0)
    fine = name >= experts
    expert = jnp.where(fine, name - experts, name)
    dense = jnp.zeros((columns, tokens), jnp.float32)
    for k in range(chosen.shape[0]):
        dense += jnp.where(chosen[k : k + 1, :] == expert, gate[k : k + 1, :], 0.0)
    coarse = dense.astype(jnp.bfloat16).astype(jnp.float32)
    both = jnp.where(fine, dense - coarse, coarse).astype(jnp.bfloat16)
    row = lax.broadcasted_iota(jnp.int32, (columns, columns), 0)
    unit = (row == lax.broadcasted_iota(jnp.int32, (columns, columns), 1)).astype(jnp.bfloat16)
    turned = lax.dot_general(both, unit, (((0,), (0,)), ((), ())), preferred_element_type=jnp.float32)
    out[...] = turned.astype(jnp.bfloat16)


def attend_kernel(
    heads,
    unroll,
    experts,
    table,
    length,
    q_ref,
    pages,
    proj,
    chosen,
    logits,
    out_wide,
    out_sent,
    out_gates,
    kbuf,
    vbuf,
    wbuf,
    qs,
    os,
    sem,
):
    tokens = q_ref.shape[0]
    per_token = table.shape[0]
    lanes = kbuf.shape[2]
    positions = per_token * kbuf.shape[1]
    copies = [
        pltpu.make_async_copy(pages.at[0], kbuf, sem.at[0]),
        pltpu.make_async_copy(pages.at[1], vbuf, sem.at[1]),
        pltpu.make_async_copy(proj, wbuf, sem.at[2]),
    ]
    for copy in copies:
        copy.start()
    low = lax.broadcasted_iota(jnp.int32, (tokens, lanes), 1) < HEAD_WIDTH
    half = heads // 2
    for h in range(heads):
        pair = q_ref[:, (h // 2) * lanes : (h // 2 + 1) * lanes].astype(jnp.float32)
        if (h < half) != (h % 2 == 0):
            pair = pltpu.roll(pair, HEAD_WIDTH, 1)
        row = jnp.where(low if h < half else ~low, pair, 0.0)
        qs[pl.ds(h, tokens, stride=heads), :] = row * (1.0 / math.sqrt(HEAD_WIDTH))
    dense_gates(experts, chosen, logits, out_gates)
    copies[0].wait()
    copies[1].wait()
    spot = lax.broadcasted_iota(jnp.int32, (heads, positions), 1)

    @pl.loop(0, tokens // unroll)
    def _(step):
        scores, values = [], []
        for u in range(unroll):
            t = step * unroll + u
            ids = [table[i, t] for i in range(per_token)]
            keys = jnp.concatenate([kbuf[i] for i in ids], axis=0)
            values.append(jnp.concatenate([vbuf[i] for i in ids], axis=0))
            q = qs[pl.ds(pl.multiple_of(t * heads, heads), heads), :].astype(jnp.bfloat16)
            s = lax.dot_general(
                q, keys, (((1,), (1,)), ((), ())), preferred_element_type=jnp.float32
            )
            scores.append(jnp.where(spot < length[t], s, -jnp.inf))
        s = jnp.concatenate(scores, axis=0)
        w = jnp.exp(s - jnp.max(s, axis=1, keepdims=True))
        total = jnp.sum(w, axis=1, keepdims=True)
        p = w.astype(jnp.bfloat16)
        o = jnp.concatenate(
            [
                jnp.dot(p[u * heads : (u + 1) * heads], values[u], preferred_element_type=jnp.float32)
                for u in range(unroll)
            ],
            axis=0,
        )
        rows = unroll * heads
        os[pl.ds(pl.multiple_of(step * rows, rows), rows), :] = o / total

    parts = []
    for j in range(half):
        even = os[pl.ds(2 * j, tokens, stride=heads), :]
        odd = os[pl.ds(2 * j + 1, tokens, stride=heads), :]
        if 2 * j < half:
            odd = pltpu.roll(odd, HEAD_WIDTH, 1)
        else:
            even = pltpu.roll(even, HEAD_WIDTH, 1)
        parts.append(jnp.where(low, even, odd).astype(jnp.bfloat16))
    attended = jnp.concatenate(parts, axis=1)
    copies[2].wait()
    part = lax.dot_general(
        attended, wbuf[...], (((1,), (1,)), ((), ())), preferred_element_type=jnp.float32
    )
    out_wide[...] = part
    out_sent[...] = part.astype(jnp.bfloat16)


def attend(query, pages, page_table, ctx_len, out_proj, chosen, logits, experts):
    tokens = query.shape[0]
    heads = query.shape[1] // HEAD_WIDTH
    width = out_proj.shape[1]
    lanes = pages.shape[3]
    rows = (tokens * heads, lanes)
    operands = (page_table.T, ctx_len, query, pages, out_proj.T, chosen.T, logits.T)
    operands = [pltpu.with_memory_space_constraint(v, pltpu.HBM) for v in operands]
    return pl.pallas_call(
        functools.partial(attend_kernel, heads, min(16, tokens), experts),
        out_shape=(
            jax.ShapeDtypeStruct((tokens, width), jnp.float32),
            jax.ShapeDtypeStruct((tokens, width), jnp.bfloat16),
            jax.ShapeDtypeStruct((tokens, 2 * experts), jnp.bfloat16),
        ),
        in_specs=[SMEM, SMEM, VMEM, HBM, HBM, VMEM, VMEM],
        out_specs=(VMEM,) * 3,
        scratch_shapes=[
            pltpu.VMEM(pages.shape[1:], pages.dtype),
            pltpu.VMEM(pages.shape[1:], pages.dtype),
            pltpu.VMEM(out_proj.shape[::-1], out_proj.dtype),
            pltpu.VMEM(rows, jnp.float32),
            pltpu.VMEM(rows, jnp.float32),
            pltpu.SemaphoreType.DMA((3,)),
        ],
        compiler_params=pltpu.CompilerParams(vmem_limit_bytes=50 * MIB),
        name="attend",
    )(*operands)


def norm_kernel(resid, own, other, gain, gates, stream_out, all_out, mine_out):
    tokens, width = own.shape
    side = lax.axis_index("tp")
    half_cols = stream_out.shape[1]
    stream = resid[...].astype(jnp.float32) + own[...] + other[...].astype(jnp.float32)
    mean_square = jnp.sum(stream * stream, axis=1, keepdims=True) / width
    normed = stream * lax.rsqrt(mean_square + 1e-05) * gain[...]
    all_out[:, :width] = normed.astype(jnp.bfloat16)
    all_out[:, width : width + gates.shape[1]] = gates[...]
    rows = tokens // 2
    mine_out[...] = all_out[pl.ds(pl.multiple_of(side * rows, rows), rows), :]
    stream_out[...] = jnp.where(side == 0, stream[:, :half_cols], stream[:, half_cols:])


def norm(resid, own, other, gain, gates, padded):
    tokens, width = own.shape
    return pl.pallas_call(
        norm_kernel,
        out_shape=(
            jax.ShapeDtypeStruct((tokens, width // 2), jnp.float32),
            jax.ShapeDtypeStruct((tokens, padded), jnp.bfloat16),
            jax.ShapeDtypeStruct((tokens // 2, padded), jnp.bfloat16),
        ),
        in_specs=[VMEM] * 5,
        out_specs=(VMEM,) * 3,
        compiler_params=pltpu.CompilerParams(vmem_limit_bytes=4 * MIB),
        name="norm",
    )(resid, own, other, gain[None], gates)


def expert_kernel(experts, pieces, *refs):
    sources = refs[:pieces]
    w_gate, w_up, w_down, keep_out, send_out, xs = refs[pieces:]
    side = lax.axis_index("tp")
    me = lax.axis_index("ep")
    width = w_gate.shape[0]
    if pieces == 1:
        xs = sources[0]
    else:
        rows = sources[0].shape[0]
        for b in range(pieces // 2):
            here = pl.multiple_of(b * 2 * rows + side * rows, rows)
            there = pl.multiple_of(b * 2 * rows + (1 - side) * rows, rows)
            xs[pl.ds(here, rows), :] = sources[2 * b][...]
            xs[pl.ds(there, rows), :] = sources[2 * b + 1][...]
    x = xs[:, :width]
    spare = xs[:, width : width + 2 * experts].astype(jnp.float32)
    column = lax.broadcasted_iota(jnp.int32, spare.shape, 1)
    mine = (column == me) | (column == me + experts)
    gate = jnp.sum(jnp.where(mine, spare, 0.0), axis=1, keepdims=True)
    g = jnp.dot(x, w_gate[...], preferred_element_type=jnp.float32)
    u = jnp.dot(x, w_up[...], preferred_element_type=jnp.float32)
    hidden = (g * jax.nn.sigmoid(1.702 * g) * (u + 1.0)).astype(jnp.bfloat16)
    y = jnp.dot(hidden, w_down[...], preferred_element_type=jnp.float32) * gate
    half_cols = y.shape[1] // 2
    left, right = y[:, :half_cols], y[:, half_cols:]
    keep_out[:, :half_cols] = jnp.where(side == 0, left, right)
    send_out[:, :half_cols] = jnp.where(side == 0, right, left).astype(jnp.bfloat16)


def expert(sources, w_gate, w_up, w_down, experts):
    pieces = len(sources)
    rows = sum(s.shape[0] for s in sources)
    padded = sources[0].shape[1]
    out_cols = -(-w_down.shape[1] // 2 // LANES) * LANES
    return pl.pallas_call(
        functools.partial(expert_kernel, experts, pieces),
        out_shape=(
            jax.ShapeDtypeStruct((rows, out_cols), jnp.float32),
            jax.ShapeDtypeStruct((rows, out_cols), jnp.bfloat16),
        ),
        in_specs=[VMEM] * (pieces + 3),
        out_specs=(VMEM,) * 2,
        scratch_shapes=[pltpu.VMEM((rows if pieces > 1 else 16, padded), jnp.bfloat16)],
        compiler_params=pltpu.CompilerParams(vmem_limit_bytes=16 * MIB),
        cost_estimate=pl.CostEstimate(
            flops=6 * rows * w_down.size, transcendentals=0, bytes_accessed=6 * w_down.size
        ),
        name="expert",
    )(*sources, w_gate, w_up, w_down)


def flip(value, axis, offset):
    return lax.ppermute(value, axis, [(i, i ^ offset) for i in range(lax.axis_size(axis))])


def step_from(k, owners):
    return 0 if k == owners - 1 else k & (k - 1)


def routed_all(stream, whole, mine, w_gate, w_up, w_down, experts):
    owners = lax.axis_size("ep")
    tokens = whole.shape[0]
    near = [k for k in range(1, owners) if k & (k - 1) == 0]
    far = [k for k in range(1, owners) if k not in near]
    half = {0: mine}
    for k in sorted(near, reverse=True) + sorted(far, key=lambda k: (k.bit_count(), -k)):
        source = step_from(k, owners)
        half[k] = flip(half[source], "ep", k ^ source)
    total = {}
    for name, group in (("own", [0]), ("near", near), ("far", far)):
        sources = [whole]
        if name != "own":
            sources = []
            for k in group:
                sources += [half[k], flip(half[k], "tp", 1)]
        kept, sent = expert(sources, w_gate[0], w_up[0], w_down[0], experts)
        received = flip(sent, "tp", 1)
        for i, k in enumerate(group):
            rows = slice(i * tokens, (i + 1) * tokens)
            total[k] = kept[rows] + received[rows].astype(jnp.float32)
    for k in sorted(range(1, owners), key=lambda k: (-k.bit_count(), -k)):
        target = step_from(k, owners)
        part = flip(total[k].astype(jnp.bfloat16), "ep", k ^ target)
        total[target] = total[target] + part.astype(jnp.float32)
    return (stream + total[0][:, : stream.shape[1]]).astype(jnp.bfloat16)


def routed_slots(stream, normed, experts_chosen, router_logits, w_gate, w_up, w_down, capacity):
    tok_rows, top_count = experts_chosen.shape
    local_experts = w_gate.shape[0]
    owners = lax.axis_size("ep")
    experts = local_experts * owners
    gate_weights = jax.nn.softmax(router_logits, axis=1)
    chosen_flat = experts_chosen.reshape(-1)
    onehot = (chosen_flat[:, None] == jnp.arange(experts, dtype=jnp.int32)[None, :]).astype(
        jnp.int32
    )
    before = jnp.cumsum(onehot, axis=0, dtype=jnp.int32) - onehot
    slot_rank = jnp.sum(before * onehot, axis=1, dtype=jnp.int32)
    slot_index = (chosen_flat * capacity + slot_rank).reshape(tok_rows, top_count)
    slot_range = jnp.arange(experts * capacity, dtype=jnp.int32)
    placed = slot_index[:, :, None] == slot_range[None, None, :]
    dispatch = jnp.sum(placed.astype(jnp.float32), axis=1).astype(jnp.bfloat16)
    outgoing = lax.dot_general(
        dispatch, normed, (((0,), (0,)), ((), ())), preferred_element_type=jnp.float32
    )
    outgoing = outgoing.astype(jnp.bfloat16).reshape(
        owners, local_experts, capacity, normed.shape[1]
    )
    arrived_full = lax.all_gather(
        lax.all_to_all(outgoing, "ep", split_axis=0, concat_axis=0, tiled=True),
        "tp",
        axis=3,
        tiled=True,
    )
    gate_value = jnp.einsum(
        "sekd,edf->sekf", arrived_full, w_gate, preferred_element_type=jnp.float32
    )
    up_value = jnp.einsum("sekd,edf->sekf", arrived_full, w_up, preferred_element_type=jnp.float32)
    hidden = (gate_value * jax.nn.sigmoid(1.702 * gate_value) * (up_value + 1.0)).astype(
        jnp.bfloat16
    )
    partial_value = jnp.einsum("sekf,efd->sekd", hidden, w_down, preferred_element_type=jnp.float32)
    finished = lax.psum_scatter(partial_value, "tp", scatter_dimension=3, tiled=True).astype(
        jnp.bfloat16
    )
    returned = lax.all_to_all(finished, "ep", split_axis=0, concat_axis=0, tiled=True)
    combine = jnp.sum(placed.astype(jnp.float32) * gate_weights[:, :, None], axis=1)
    expert_mix = jnp.dot(
        combine,
        returned.reshape(experts * capacity, -1).astype(jnp.float32),
        precision=lax.Precision.HIGHEST,
    )
    return (stream + expert_mix).astype(jnp.bfloat16)


def layer(
    resid,
    query,
    key_value_pages,
    page_table,
    ctx_len,
    experts_chosen,
    router_logits,
    norm_gain,
    out_proj,
    w_gate,
    w_up,
    w_down,
):
    tok_rows, model_width = resid.shape
    top_count = experts_chosen.shape[1]
    local_experts = w_gate.shape[0]
    owners = lax.axis_size("ep")
    experts = local_experts * owners
    capacity = max(2, min(tok_rows, 2 * tok_rows * top_count // experts))
    padded = -(-model_width // LANES) * LANES

    own, sent, gates = attend(
        query, key_value_pages, page_table, ctx_len, out_proj, experts_chosen, router_logits, experts
    )
    other = flip(sent, "tp", 1)
    if (
        local_experts == 1
        and tok_rows <= capacity
        and model_width + 2 * experts <= padded
        and owners & (owners - 1) == 0
    ):
        stream, whole, mine = norm(resid, own, other, norm_gain, gates, padded)
        return routed_all(stream, whole, mine, w_gate, w_up, w_down, experts)
    half_cols = model_width // lax.axis_size("tp")
    offset = lax.axis_index("tp") * half_cols
    stream = resid.astype(jnp.float32) + own + other.astype(jnp.float32)
    mean_square = jnp.mean(stream * stream, axis=1, keepdims=True)
    normed = (stream * lax.rsqrt(mean_square + 1e-05) * norm_gain).astype(jnp.bfloat16)
    stream = lax.dynamic_slice_in_dim(stream, offset, half_cols, 1)
    normed = lax.dynamic_slice_in_dim(normed, offset, half_cols, 1)
    return routed_slots(
        stream, normed, experts_chosen, router_logits, w_gate, w_up, w_down, capacity
    )


def solution(mesh):
    return jax.shard_map(
        layer,
        mesh=mesh,
        in_specs=(
            P(("rep", "ep"), None),
            P(("rep", "ep"), "tp"),
            P(None, ("rep", "ep"), None, "tp"),
            P(("rep", "ep"), None),
            P(("rep", "ep")),
            P(("rep", "ep"), None),
            P(("rep", "ep"), None),
            P(),
            P("tp", None),
            P("ep", None, "tp"),
            P("ep", None, "tp"),
            P("ep", "tp", None),
        ),
        out_specs=P(("rep", "ep"), "tp"),
        check_vma=False,
    )
```

```python
import functools
import math

import jax
import jax.numpy as jnp
from jax import lax
from jax.experimental import pallas as pl
from jax.experimental.pallas import tpu as pltpu
from jax.sharding import PartitionSpec as P


HEAD_WIDTH = 64
LANES = 128
MIB = 1 << 20
ATTEND_MIB = 36

SMEM = pl.BlockSpec(memory_space=pltpu.SMEM)
VMEM = pl.BlockSpec(memory_space=pltpu.VMEM)
HBM = pl.BlockSpec(memory_space=pltpu.HBM)


def dense_gates(experts, chosen, logits, out):
    tokens, columns = out.shape
    gate = jnp.exp(logits[...] - jnp.max(logits[...], axis=0, keepdims=True))
    gate = gate / jnp.sum(gate, axis=0, keepdims=True)
    name = lax.broadcasted_iota(jnp.int32, (columns, tokens), 0)
    fine = name >= experts
    expert = jnp.where(fine, name - experts, name)
    dense = jnp.zeros((columns, tokens), jnp.float32)
    for k in range(chosen.shape[0]):
        dense += jnp.where(chosen[k : k + 1, :] == expert, gate[k : k + 1, :], 0.0)
    coarse = dense.astype(jnp.bfloat16).astype(jnp.float32)
    both = jnp.where(fine, dense - coarse, coarse).astype(jnp.bfloat16)
    row = lax.broadcasted_iota(jnp.int32, (columns, columns), 0)
    unit = (row == lax.broadcasted_iota(jnp.int32, (columns, columns), 1)).astype(jnp.bfloat16)
    turned = lax.dot_general(both, unit, (((0,), (0,)), ((), ())), preferred_element_type=jnp.float32)
    out[...] = turned.astype(jnp.bfloat16)


def attend_kernel(
    heads,
    experts,
    table_in,
    length_in,
    q_in,
    pages,
    proj,
    chosen_in,
    logits_in,
    *refs,
):
    count = (len(refs) - 15) // 2
    weights_in, (out_wide, out_sent, out_gates) = refs[:count], refs[count : count + 3]
    weights_out, refs = refs[count + 3 : 2 * count + 3], refs[2 * count + 3 :]
    table, length, q, chosen, logits, kbuf, vbuf, wbuf, qs, ws, os, sem = refs
    tokens = q.shape[0]
    per_token = table.shape[0]
    lanes = kbuf.shape[2]
    positions = per_token * kbuf.shape[1]
    moves = (
        (q_in, q),
        (chosen_in, chosen),
        (logits_in, logits),
        (table_in, table),
        (length_in, length),
        (pages.at[0], kbuf),
        (pages.at[1], vbuf),
        (proj, wbuf),
        *zip(weights_in, weights_out),
    )
    copies = [pltpu.make_async_copy(*move, sem.at[i]) for i, move in enumerate(moves)]
    small, (keys_in, values_in, proj_in), experts_in = copies[:5], copies[5:8], copies[8:]
    for copy in copies:
        copy.start()
    small[0].wait()
    low = lax.broadcasted_iota(jnp.int32, (tokens, lanes), 1) < HEAD_WIDTH
    half = heads // 2
    for h in range(heads):
        pair = q[:, (h // 2) * lanes : (h // 2 + 1) * lanes].astype(jnp.float32)
        if (h < half) != (h % 2 == 0):
            pair = pltpu.roll(pair, HEAD_WIDTH, 1)
        row = jnp.where(low if h < half else ~low, pair, 0.0)
        qs[pl.ds(h, tokens, stride=heads), :] = row * (1.0 / math.sqrt(HEAD_WIDTH))
    for copy in small[1:]:
        copy.wait()
    dense_gates(experts, chosen, logits, out_gates)
    keys_in.wait()
    spot = lax.broadcasted_iota(jnp.int32, (heads, positions), 1)

    def tiles(buffer, t):
        return jnp.concatenate([buffer[table[i, t]] for i in range(per_token)], axis=0)

    scores = []
    for t in range(tokens):
        rows = qs[t * heads : (t + 1) * heads, :].astype(jnp.bfloat16)
        s = lax.dot_general(
            rows, tiles(kbuf, t), (((1,), (1,)), ((), ())), preferred_element_type=jnp.float32
        )
        scores.append(jnp.where(spot < length[t], s, -jnp.inf))
    s = jnp.concatenate(scores, axis=0)
    w = jnp.exp(s - jnp.max(s, axis=1, keepdims=True))
    ws[...] = (w / jnp.sum(w, axis=1, keepdims=True)).astype(jnp.bfloat16)
    values_in.wait()
    for t in range(tokens):
        rows = slice(t * heads, (t + 1) * heads)
        os[rows, :] = jnp.dot(ws[rows, :], tiles(vbuf, t), preferred_element_type=jnp.float32)

    parts = []
    for j in range(half):
        even = os[pl.ds(2 * j, tokens, stride=heads), :]
        odd = os[pl.ds(2 * j + 1, tokens, stride=heads), :]
        if 2 * j < half:
            odd = pltpu.roll(odd, HEAD_WIDTH, 1)
        else:
            even = pltpu.roll(even, HEAD_WIDTH, 1)
        parts.append(jnp.where(low, even, odd).astype(jnp.bfloat16))
    attended = jnp.concatenate(parts, axis=1)
    proj_in.wait()
    part = lax.dot_general(
        attended, wbuf[...], (((1,), (1,)), ((), ())), preferred_element_type=jnp.float32
    )
    out_wide[...] = part
    out_sent[...] = part.astype(jnp.bfloat16)
    for copy in experts_in:
        copy.wait()


def attend(query, pages, page_table, ctx_len, out_proj, chosen, logits, experts, weights):
    tokens = query.shape[0]
    heads = query.shape[1] // HEAD_WIDTH
    width = out_proj.shape[1]
    lanes = pages.shape[3]
    rows = (tokens * heads, lanes)
    operands = (page_table.T, ctx_len, query, pages, out_proj.T, chosen.T, logits.T, *weights)
    operands = [pltpu.with_memory_space_constraint(v, pltpu.HBM) for v in operands]
    return pl.pallas_call(
        functools.partial(attend_kernel, heads, experts),
        out_shape=(
            jax.ShapeDtypeStruct((tokens, width), jnp.float32),
            jax.ShapeDtypeStruct((tokens, width), jnp.bfloat16),
            jax.ShapeDtypeStruct((tokens, 2 * experts), jnp.bfloat16),
            *[jax.ShapeDtypeStruct(w.shape, w.dtype) for w in weights],
        ),
        in_specs=[HBM] * len(operands),
        out_specs=(VMEM,) * (3 + len(weights)),
        scratch_shapes=[
            pltpu.SMEM(operands[0].shape, jnp.int32),
            pltpu.SMEM(operands[1].shape, jnp.int32),
            pltpu.VMEM(query.shape, query.dtype),
            pltpu.VMEM(operands[5].shape, jnp.int32),
            pltpu.VMEM(operands[6].shape, jnp.float32),
            pltpu.VMEM(pages.shape[1:], pages.dtype),
            pltpu.VMEM(pages.shape[1:], pages.dtype),
            pltpu.VMEM(operands[4].shape, out_proj.dtype),
            pltpu.VMEM(rows, jnp.float32),
            pltpu.VMEM((rows[0], page_table.shape[1] * pages.shape[2]), jnp.bfloat16),
            pltpu.VMEM(rows, jnp.float32),
            pltpu.SemaphoreType.DMA((8 + len(weights),)),
        ],
        compiler_params=pltpu.CompilerParams(vmem_limit_bytes=ATTEND_MIB * MIB),
        name="attend",
    )(*operands)


def norm_kernel(resid, own, other, gain, gates, stream_out, all_out, mine_out):
    tokens, width = own.shape
    side = lax.axis_index("tp")
    half_cols = stream_out.shape[1]
    stream = resid[...].astype(jnp.float32) + own[...] + other[...].astype(jnp.float32)
    mean_square = jnp.sum(stream * stream, axis=1, keepdims=True) / width
    normed = stream * lax.rsqrt(mean_square + 1e-05) * gain[...]
    all_out[:, :width] = normed.astype(jnp.bfloat16)
    all_out[:, width : width + gates.shape[1]] = gates[...]
    rows = tokens // 2
    mine_out[...] = all_out[pl.ds(pl.multiple_of(side * rows, rows), rows), :]
    stream_out[...] = jnp.where(side == 0, stream[:, :half_cols], stream[:, half_cols:])


def norm(resid, own, other, gain, gates, padded):
    tokens, width = own.shape
    return pl.pallas_call(
        norm_kernel,
        out_shape=(
            jax.ShapeDtypeStruct((tokens, width // 2), jnp.float32),
            jax.ShapeDtypeStruct((tokens, padded), jnp.bfloat16),
            jax.ShapeDtypeStruct((tokens // 2, padded), jnp.bfloat16),
        ),
        in_specs=[VMEM] * 5,
        out_specs=(VMEM,) * 3,
        compiler_params=pltpu.CompilerParams(vmem_limit_bytes=4 * MIB),
        name="norm",
    )(resid, own, other, gain[None], gates)


def expert_kernel(experts, pieces, *refs):
    sources = refs[:pieces]
    w_gate, w_up, w_down, keep_out, send_out, xs = refs[pieces:]
    side = lax.axis_index("tp")
    me = lax.axis_index("ep")
    width = w_gate.shape[0]
    if pieces == 1:
        xs = sources[0]
    else:
        rows = sources[0].shape[0]
        for b in range(pieces // 2):
            here = pl.multiple_of(b * 2 * rows + side * rows, rows)
            there = pl.multiple_of(b * 2 * rows + (1 - side) * rows, rows)
            xs[pl.ds(here, rows), :] = sources[2 * b][...]
            xs[pl.ds(there, rows), :] = sources[2 * b + 1][...]
    x = xs[:, :width]
    spare = xs[:, width : width + 2 * experts].astype(jnp.float32)
    column = lax.broadcasted_iota(jnp.int32, spare.shape, 1)
    mine = (column == me) | (column == me + experts)
    gate = jnp.sum(jnp.where(mine, spare, 0.0), axis=1, keepdims=True)
    g = jnp.dot(x, w_gate[...], preferred_element_type=jnp.float32)
    u = jnp.dot(x, w_up[...], preferred_element_type=jnp.float32)
    hidden = (g * jax.nn.sigmoid(1.702 * g) * (u + 1.0)).astype(jnp.bfloat16)
    y = jnp.dot(hidden, w_down[...], preferred_element_type=jnp.float32) * gate
    half_cols = y.shape[1] // 2
    left, right = y[:, :half_cols], y[:, half_cols:]
    keep_out[:, :half_cols] = jnp.where(side == 0, left, right)
    send_out[:, :half_cols] = jnp.where(side == 0, right, left).astype(jnp.bfloat16)


def expert(sources, w_gate, w_up, w_down, experts):
    pieces = len(sources)
    rows = sum(s.shape[0] for s in sources)
    padded = sources[0].shape[1]
    out_cols = -(-w_down.shape[1] // 2 // LANES) * LANES
    return pl.pallas_call(
        functools.partial(expert_kernel, experts, pieces),
        out_shape=(
            jax.ShapeDtypeStruct((rows, out_cols), jnp.float32),
            jax.ShapeDtypeStruct((rows, out_cols), jnp.bfloat16),
        ),
        in_specs=[VMEM] * (pieces + 3),
        out_specs=(VMEM,) * 2,
        scratch_shapes=[pltpu.VMEM((rows if pieces > 1 else 16, padded), jnp.bfloat16)],
        compiler_params=pltpu.CompilerParams(vmem_limit_bytes=16 * MIB),
        cost_estimate=pl.CostEstimate(
            flops=6 * rows * w_down.size, transcendentals=0, bytes_accessed=6 * w_down.size
        ),
        name="expert",
    )(*sources, w_gate, w_up, w_down)


def flip(value, axis, offset):
    return lax.ppermute(value, axis, [(i, i ^ offset) for i in range(lax.axis_size(axis))])


def step_from(k, owners):
    return 0 if k == owners - 1 else k & (k - 1)


def routed_all(stream, whole, mine, weights, experts):
    owners = lax.axis_size("ep")
    tokens = whole.shape[0]
    near = [k for k in range(1, owners) if k & (k - 1) == 0]
    far = [k for k in range(1, owners) if k not in near]
    half = {0: mine}
    for k in sorted(near, reverse=True) + sorted(far, key=lambda k: (k.bit_count(), -k)):
        source = step_from(k, owners)
        half[k] = flip(half[source], "ep", k ^ source)
    total = {}
    for name, group in (("own", [0]), ("near", near), ("far", far)):
        sources = [whole]
        if name != "own":
            sources = []
            for k in group:
                sources += [half[k], flip(half[k], "tp", 1)]
        kept, sent = expert(sources, *weights, experts)
        received = flip(sent, "tp", 1)
        for i, k in enumerate(group):
            rows = slice(i * tokens, (i + 1) * tokens)
            total[k] = kept[rows] + received[rows].astype(jnp.float32)
    for k in sorted(range(1, owners), key=lambda k: (-k.bit_count(), -k)):
        target = step_from(k, owners)
        part = flip(total[k].astype(jnp.bfloat16), "ep", k ^ target)
        total[target] = total[target] + part.astype(jnp.float32)
    return (stream + total[0][:, : stream.shape[1]]).astype(jnp.bfloat16)


def routed_slots(stream, normed, experts_chosen, router_logits, w_gate, w_up, w_down, capacity):
    tok_rows, top_count = experts_chosen.shape
    local_experts = w_gate.shape[0]
    owners = lax.axis_size("ep")
    experts = local_experts * owners
    gate_weights = jax.nn.softmax(router_logits, axis=1)
    chosen_flat = experts_chosen.reshape(-1)
    onehot = (chosen_flat[:, None] == jnp.arange(experts, dtype=jnp.int32)[None, :]).astype(
        jnp.int32
    )
    before = jnp.cumsum(onehot, axis=0, dtype=jnp.int32) - onehot
    slot_rank = jnp.sum(before * onehot, axis=1, dtype=jnp.int32)
    slot_index = (chosen_flat * capacity + slot_rank).reshape(tok_rows, top_count)
    slot_range = jnp.arange(experts * capacity, dtype=jnp.int32)
    placed = slot_index[:, :, None] == slot_range[None, None, :]
    dispatch = jnp.sum(placed.astype(jnp.float32), axis=1).astype(jnp.bfloat16)
    outgoing = lax.dot_general(
        dispatch, normed, (((0,), (0,)), ((), ())), preferred_element_type=jnp.float32
    )
    outgoing = outgoing.astype(jnp.bfloat16).reshape(
        owners, local_experts, capacity, normed.shape[1]
    )
    arrived_full = lax.all_gather(
        lax.all_to_all(outgoing, "ep", split_axis=0, concat_axis=0, tiled=True),
        "tp",
        axis=3,
        tiled=True,
    )
    gate_value = jnp.einsum(
        "sekd,edf->sekf", arrived_full, w_gate, preferred_element_type=jnp.float32
    )
    up_value = jnp.einsum("sekd,edf->sekf", arrived_full, w_up, preferred_element_type=jnp.float32)
    hidden = (gate_value * jax.nn.sigmoid(1.702 * gate_value) * (up_value + 1.0)).astype(
        jnp.bfloat16
    )
    partial_value = jnp.einsum("sekf,efd->sekd", hidden, w_down, preferred_element_type=jnp.float32)
    finished = lax.psum_scatter(partial_value, "tp", scatter_dimension=3, tiled=True).astype(
        jnp.bfloat16
    )
    returned = lax.all_to_all(finished, "ep", split_axis=0, concat_axis=0, tiled=True)
    combine = jnp.sum(placed.astype(jnp.float32) * gate_weights[:, :, None], axis=1)
    expert_mix = jnp.dot(
        combine,
        returned.reshape(experts * capacity, -1).astype(jnp.float32),
        precision=lax.Precision.HIGHEST,
    )
    return (stream + expert_mix).astype(jnp.bfloat16)


def layer(
    resid,
    query,
    key_value_pages,
    page_table,
    ctx_len,
    experts_chosen,
    router_logits,
    norm_gain,
    out_proj,
    w_gate,
    w_up,
    w_down,
):
    tok_rows, model_width = resid.shape
    top_count = experts_chosen.shape[1]
    local_experts = w_gate.shape[0]
    owners = lax.axis_size("ep")
    experts = local_experts * owners
    capacity = max(2, min(tok_rows, 2 * tok_rows * top_count // experts))
    padded = -(-model_width // LANES) * LANES

    dense = (
        local_experts == 1
        and tok_rows <= capacity
        and model_width + 2 * experts <= padded
        and owners & (owners - 1) == 0
    )
    own, sent, gates, *weights = attend(
        query,
        key_value_pages,
        page_table,
        ctx_len,
        out_proj,
        experts_chosen,
        router_logits,
        experts,
        (w_gate[0], w_up[0], w_down[0]) if dense else (),
    )
    other = flip(sent, "tp", 1)
    if dense:
        stream, whole, mine = norm(resid, own, other, norm_gain, gates, padded)
        return routed_all(stream, whole, mine, weights, experts)
    half_cols = model_width // lax.axis_size("tp")
    offset = lax.axis_index("tp") * half_cols
    stream = resid.astype(jnp.float32) + own + other.astype(jnp.float32)
    mean_square = jnp.mean(stream * stream, axis=1, keepdims=True)
    normed = (stream * lax.rsqrt(mean_square + 1e-05) * norm_gain).astype(jnp.bfloat16)
    stream = lax.dynamic_slice_in_dim(stream, offset, half_cols, 1)
    normed = lax.dynamic_slice_in_dim(normed, offset, half_cols, 1)
    return routed_slots(
        stream, normed, experts_chosen, router_logits, w_gate, w_up, w_down, capacity
    )


def solution(mesh):
    return jax.shard_map(
        layer,
        mesh=mesh,
        in_specs=(
            P(("rep", "ep"), None),
            P(("rep", "ep"), "tp"),
            P(None, ("rep", "ep"), None, "tp"),
            P(("rep", "ep"), None),
            P(("rep", "ep")),
            P(("rep", "ep"), None),
            P(("rep", "ep"), None),
            P(),
            P("tp", None),
            P("ep", None, "tp"),
            P("ep", None, "tp"),
            P("ep", "tp", None),
        ),
        out_specs=P(("rep", "ep"), "tp"),
        check_vma=False,
    )
```

```python
import functools
import math

import jax
import jax.numpy as jnp
from jax import lax
from jax.experimental import pallas as pl
from jax.experimental.pallas import tpu as pltpu
from jax.sharding import PartitionSpec as P


HEAD_WIDTH = 64
LANES = 128
MIB = 1 << 20
ATTEND_MIB = 36

SMEM = pl.BlockSpec(memory_space=pltpu.SMEM)
VMEM = pl.BlockSpec(memory_space=pltpu.VMEM)
HBM = pl.BlockSpec(memory_space=pltpu.HBM)


def dense_gates(experts, chosen, logits, out):
    tokens, columns = out.shape
    gate = jnp.exp(logits[...] - jnp.max(logits[...], axis=0, keepdims=True))
    gate = gate / jnp.sum(gate, axis=0, keepdims=True)
    name = lax.broadcasted_iota(jnp.int32, (columns, tokens), 0)
    fine = name >= experts
    expert = jnp.where(fine, name - experts, name)
    dense = jnp.zeros((columns, tokens), jnp.float32)
    for k in range(chosen.shape[0]):
        dense += jnp.where(chosen[k : k + 1, :] == expert, gate[k : k + 1, :], 0.0)
    coarse = dense.astype(jnp.bfloat16).astype(jnp.float32)
    both = jnp.where(fine, dense - coarse, coarse).astype(jnp.bfloat16)
    row = lax.broadcasted_iota(jnp.int32, (columns, columns), 0)
    unit = (row == lax.broadcasted_iota(jnp.int32, (columns, columns), 1)).astype(jnp.bfloat16)
    turned = lax.dot_general(both, unit, (((0,), (0,)), ((), ())), preferred_element_type=jnp.float32)
    out[...] = turned.astype(jnp.bfloat16)


def attend_kernel(
    heads,
    experts,
    table_in,
    length_in,
    q_in,
    pages,
    proj,
    chosen_in,
    logits_in,
    *refs,
):
    count = (len(refs) - 15) // 2
    weights_in, (out_wide, out_sent, out_gates) = refs[:count], refs[count : count + 3]
    weights_out, refs = refs[count + 3 : 2 * count + 3], refs[2 * count + 3 :]
    table, length, q, chosen, logits, kbuf, vbuf, wbuf, qs, ws, os, sem = refs
    tokens = q.shape[0]
    per_token = table.shape[0]
    lanes = kbuf.shape[2]
    positions = per_token * kbuf.shape[1]
    moves = (
        (q_in, q),
        (chosen_in, chosen),
        (logits_in, logits),
        (table_in, table),
        (length_in, length),
        (pages.at[0], kbuf),
        (pages.at[1], vbuf),
        (proj, wbuf),
        *zip(weights_in, weights_out),
    )
    copies = [pltpu.make_async_copy(*move, sem.at[i]) for i, move in enumerate(moves)]
    small, (keys_in, values_in, proj_in), experts_in = copies[:5], copies[5:8], copies[8:]
    for copy in copies:
        copy.start()
    small[0].wait()
    low = lax.broadcasted_iota(jnp.int32, (tokens, lanes), 1) < HEAD_WIDTH
    half = heads // 2
    for h in range(heads):
        pair = q[:, (h // 2) * lanes : (h // 2 + 1) * lanes].astype(jnp.float32)
        if (h < half) != (h % 2 == 0):
            pair = pltpu.roll(pair, HEAD_WIDTH, 1)
        row = jnp.where(low if h < half else ~low, pair, 0.0)
        qs[pl.ds(h, tokens, stride=heads), :] = row * (1.0 / math.sqrt(HEAD_WIDTH))
    for copy in small[1:]:
        copy.wait()
    dense_gates(experts, chosen, logits, out_gates)
    keys_in.wait()
    spot = lax.broadcasted_iota(jnp.int32, (heads, positions), 1)

    def tiles(buffer, t):
        return jnp.concatenate([buffer[table[i, t]] for i in range(per_token)], axis=0)

    scores = []
    for t in range(tokens):
        rows = qs[t * heads : (t + 1) * heads, :].astype(jnp.bfloat16)
        s = lax.dot_general(
            rows, tiles(kbuf, t), (((1,), (1,)), ((), ())), preferred_element_type=jnp.float32
        )
        scores.append(jnp.where(spot < length[t], s, -jnp.inf))
    s = jnp.concatenate(scores, axis=0)
    w = jnp.exp(s - jnp.max(s, axis=1, keepdims=True))
    ws[...] = (w / jnp.sum(w, axis=1, keepdims=True)).astype(jnp.bfloat16)
    values_in.wait()
    for t in range(tokens):
        rows = slice(t * heads, (t + 1) * heads)
        os[rows, :] = jnp.dot(ws[rows, :], tiles(vbuf, t), preferred_element_type=jnp.float32)

    parts = []
    for j in range(half):
        even = os[pl.ds(2 * j, tokens, stride=heads), :]
        odd = os[pl.ds(2 * j + 1, tokens, stride=heads), :]
        if 2 * j < half:
            odd = pltpu.roll(odd, HEAD_WIDTH, 1)
        else:
            even = pltpu.roll(even, HEAD_WIDTH, 1)
        parts.append(jnp.where(low, even, odd).astype(jnp.bfloat16))
    attended = jnp.concatenate(parts, axis=1)
    proj_in.wait()
    part = lax.dot_general(
        attended, wbuf[...], (((1,), (1,)), ((), ())), preferred_element_type=jnp.float32
    )
    out_wide[...] = part
    out_sent[...] = part.astype(jnp.bfloat16)
    for copy in experts_in:
        copy.wait()


def attend(query, pages, page_table, ctx_len, out_proj, chosen, logits, experts, weights):
    tokens = query.shape[0]
    heads = query.shape[1] // HEAD_WIDTH
    width = out_proj.shape[1]
    lanes = pages.shape[3]
    rows = (tokens * heads, lanes)
    operands = (page_table.T, ctx_len, query, pages, out_proj.T, chosen.T, logits.T, *weights)
    operands = [pltpu.with_memory_space_constraint(v, pltpu.HBM) for v in operands]
    return pl.pallas_call(
        functools.partial(attend_kernel, heads, experts),
        out_shape=(
            jax.ShapeDtypeStruct((tokens, width), jnp.float32),
            jax.ShapeDtypeStruct((tokens, width), jnp.bfloat16),
            jax.ShapeDtypeStruct((tokens, 2 * experts), jnp.bfloat16),
            *[jax.ShapeDtypeStruct(w.shape, w.dtype) for w in weights],
        ),
        in_specs=[HBM] * len(operands),
        out_specs=(VMEM,) * (3 + len(weights)),
        scratch_shapes=[
            pltpu.SMEM(operands[0].shape, jnp.int32),
            pltpu.SMEM(operands[1].shape, jnp.int32),
            pltpu.VMEM(query.shape, query.dtype),
            pltpu.VMEM(operands[5].shape, jnp.int32),
            pltpu.VMEM(operands[6].shape, jnp.float32),
            pltpu.VMEM(pages.shape[1:], pages.dtype),
            pltpu.VMEM(pages.shape[1:], pages.dtype),
            pltpu.VMEM(operands[4].shape, out_proj.dtype),
            pltpu.VMEM(rows, jnp.float32),
            pltpu.VMEM((rows[0], page_table.shape[1] * pages.shape[2]), jnp.bfloat16),
            pltpu.VMEM(rows, jnp.float32),
            pltpu.SemaphoreType.DMA((8 + len(weights),)),
        ],
        compiler_params=pltpu.CompilerParams(vmem_limit_bytes=ATTEND_MIB * MIB),
        name="attend",
    )(*operands)


def norm_kernel(resid, own, other, gain, gates, stream_out, all_out, mine_out):
    tokens, width = own.shape
    side = lax.axis_index("tp")
    half_cols = stream_out.shape[1]
    stream = resid[...].astype(jnp.float32) + own[...] + other[...].astype(jnp.float32)
    mean_square = jnp.sum(stream * stream, axis=1, keepdims=True) / width
    normed = stream * lax.rsqrt(mean_square + 1e-05) * gain[...]
    all_out[:, :width] = normed.astype(jnp.bfloat16)
    all_out[:, width : width + gates.shape[1]] = gates[...]
    rows = tokens // 2
    mine_out[...] = all_out[pl.ds(pl.multiple_of(side * rows, rows), rows), :]
    stream_out[...] = jnp.where(side == 0, stream[:, :half_cols], stream[:, half_cols:])


def norm(resid, own, other, gain, gates, padded):
    tokens, width = own.shape
    return pl.pallas_call(
        norm_kernel,
        out_shape=(
            jax.ShapeDtypeStruct((tokens, width // 2), jnp.float32),
            jax.ShapeDtypeStruct((tokens, padded), jnp.bfloat16),
            jax.ShapeDtypeStruct((tokens // 2, padded), jnp.bfloat16),
        ),
        in_specs=[VMEM] * 5,
        out_specs=(VMEM,) * 3,
        compiler_params=pltpu.CompilerParams(vmem_limit_bytes=4 * MIB),
        name="norm",
    )(resid, own, other, gain[None], gates)


def expert_kernel(experts, pieces, *refs):
    sources = refs[:pieces]
    w_gate, w_up, w_down, keep_out, send_out, xs = refs[pieces:]
    side = lax.axis_index("tp")
    me = lax.axis_index("ep")
    width = w_gate.shape[0]
    if pieces == 1:
        xs = sources[0]
    else:
        rows = sources[0].shape[0]
        for b in range(pieces // 2):
            here = pl.multiple_of(b * 2 * rows + side * rows, rows)
            there = pl.multiple_of(b * 2 * rows + (1 - side) * rows, rows)
            xs[pl.ds(here, rows), :] = sources[2 * b][...]
            xs[pl.ds(there, rows), :] = sources[2 * b + 1][...]
    x = xs[:, :width]
    spare = xs[:, width : width + 2 * experts].astype(jnp.float32)
    column = lax.broadcasted_iota(jnp.int32, spare.shape, 1)
    mine = (column == me) | (column == me + experts)
    gate = jnp.sum(jnp.where(mine, spare, 0.0), axis=1, keepdims=True)
    g = jnp.dot(x, w_gate[...], preferred_element_type=jnp.float32)
    u = jnp.dot(x, w_up[...], preferred_element_type=jnp.float32)
    hidden = (g * jax.nn.sigmoid(1.702 * g) * (u + 1.0)).astype(jnp.bfloat16)
    y = jnp.dot(hidden, w_down[...], preferred_element_type=jnp.float32) * gate
    half_cols = y.shape[1] // 2
    left, right = y[:, :half_cols], y[:, half_cols:]
    keep_out[:, :half_cols] = jnp.where(side == 0, left, right)
    send_out[:, :half_cols] = jnp.where(side == 0, right, left).astype(jnp.bfloat16)


def expert(sources, w_gate, w_up, w_down, experts):
    pieces = len(sources)
    rows = sum(s.shape[0] for s in sources)
    padded = sources[0].shape[1]
    out_cols = -(-w_down.shape[1] // 2 // LANES) * LANES
    return pl.pallas_call(
        functools.partial(expert_kernel, experts, pieces),
        out_shape=(
            jax.ShapeDtypeStruct((rows, out_cols), jnp.float32),
            jax.ShapeDtypeStruct((rows, out_cols), jnp.bfloat16),
        ),
        in_specs=[VMEM] * (pieces + 3),
        out_specs=(VMEM,) * 2,
        scratch_shapes=[pltpu.VMEM((rows if pieces > 1 else 16, padded), jnp.bfloat16)],
        compiler_params=pltpu.CompilerParams(vmem_limit_bytes=16 * MIB),
        cost_estimate=pl.CostEstimate(
            flops=6 * rows * w_down.size, transcendentals=0, bytes_accessed=6 * w_down.size
        ),
        name="expert",
    )(*sources, w_gate, w_up, w_down)


def flip(value, axis, offset):
    return lax.ppermute(value, axis, [(i, i ^ offset) for i in range(lax.axis_size(axis))])


def step_from(k):
    top = 1 << (k.bit_length() - 1)
    return 0 if k == top else top


def routed_all(stream, whole, mine, weights, experts):
    owners = lax.axis_size("ep")
    tokens = whole.shape[0]
    near = [k for k in range(1, owners) if k & (k - 1) == 0]
    far = [k for k in range(1, owners) if k not in near]
    half = {0: mine}
    for k in sorted(near, reverse=True) + far:
        source = step_from(k)
        half[k] = flip(half[source], "ep", k ^ source)
    total = {}
    for name, group in (("own", [0]), ("near", near), ("far", far)):
        sources = [whole]
        if name != "own":
            sources = []
            for k in group:
                sources += [half[k], flip(half[k], "tp", 1)]
        kept, sent = expert(sources, *weights, experts)
        received = flip(sent, "tp", 1)
        for i, k in enumerate(group):
            rows = slice(i * tokens, (i + 1) * tokens)
            total[k] = kept[rows] + received[rows].astype(jnp.float32)
    for k in far + near:
        target = step_from(k)
        part = flip(total[k].astype(jnp.bfloat16), "ep", k ^ target)
        total[target] = total[target] + part.astype(jnp.float32)
    return (stream + total[0][:, : stream.shape[1]]).astype(jnp.bfloat16)


def routed_slots(stream, normed, experts_chosen, router_logits, w_gate, w_up, w_down, capacity):
    tok_rows, top_count = experts_chosen.shape
    local_experts = w_gate.shape[0]
    owners = lax.axis_size("ep")
    experts = local_experts * owners
    gate_weights = jax.nn.softmax(router_logits, axis=1)
    chosen_flat = experts_chosen.reshape(-1)
    onehot = (chosen_flat[:, None] == jnp.arange(experts, dtype=jnp.int32)[None, :]).astype(
        jnp.int32
    )
    before = jnp.cumsum(onehot, axis=0, dtype=jnp.int32) - onehot
    slot_rank = jnp.sum(before * onehot, axis=1, dtype=jnp.int32)
    slot_index = (chosen_flat * capacity + slot_rank).reshape(tok_rows, top_count)
    slot_range = jnp.arange(experts * capacity, dtype=jnp.int32)
    placed = slot_index[:, :, None] == slot_range[None, None, :]
    dispatch = jnp.sum(placed.astype(jnp.float32), axis=1).astype(jnp.bfloat16)
    outgoing = lax.dot_general(
        dispatch, normed, (((0,), (0,)), ((), ())), preferred_element_type=jnp.float32
    )
    outgoing = outgoing.astype(jnp.bfloat16).reshape(
        owners, local_experts, capacity, normed.shape[1]
    )
    arrived_full = lax.all_gather(
        lax.all_to_all(outgoing, "ep", split_axis=0, concat_axis=0, tiled=True),
        "tp",
        axis=3,
        tiled=True,
    )
    gate_value = jnp.einsum(
        "sekd,edf->sekf", arrived_full, w_gate, preferred_element_type=jnp.float32
    )
    up_value = jnp.einsum("sekd,edf->sekf", arrived_full, w_up, preferred_element_type=jnp.float32)
    hidden = (gate_value * jax.nn.sigmoid(1.702 * gate_value) * (up_value + 1.0)).astype(
        jnp.bfloat16
    )
    partial_value = jnp.einsum("sekf,efd->sekd", hidden, w_down, preferred_element_type=jnp.float32)
    finished = lax.psum_scatter(partial_value, "tp", scatter_dimension=3, tiled=True).astype(
        jnp.bfloat16
    )
    returned = lax.all_to_all(finished, "ep", split_axis=0, concat_axis=0, tiled=True)
    combine = jnp.sum(placed.astype(jnp.float32) * gate_weights[:, :, None], axis=1)
    expert_mix = jnp.dot(
        combine,
        returned.reshape(experts * capacity, -1).astype(jnp.float32),
        precision=lax.Precision.HIGHEST,
    )
    return (stream + expert_mix).astype(jnp.bfloat16)


def layer(
    resid,
    query,
    key_value_pages,
    page_table,
    ctx_len,
    experts_chosen,
    router_logits,
    norm_gain,
    out_proj,
    w_gate,
    w_up,
    w_down,
):
    tok_rows, model_width = resid.shape
    top_count = experts_chosen.shape[1]
    local_experts = w_gate.shape[0]
    owners = lax.axis_size("ep")
    experts = local_experts * owners
    capacity = max(2, min(tok_rows, 2 * tok_rows * top_count // experts))
    padded = -(-model_width // LANES) * LANES

    dense = (
        local_experts == 1
        and tok_rows <= capacity
        and model_width + 2 * experts <= padded
        and owners & (owners - 1) == 0
    )
    own, sent, gates, *weights = attend(
        query,
        key_value_pages,
        page_table,
        ctx_len,
        out_proj,
        experts_chosen,
        router_logits,
        experts,
        (w_gate[0], w_up[0], w_down[0]) if dense else (),
    )
    other = flip(sent, "tp", 1)
    if dense:
        stream, whole, mine = norm(resid, own, other, norm_gain, gates, padded)
        return routed_all(stream, whole, mine, weights, experts)
    half_cols = model_width // lax.axis_size("tp")
    offset = lax.axis_index("tp") * half_cols
    stream = resid.astype(jnp.float32) + own + other.astype(jnp.float32)
    mean_square = jnp.mean(stream * stream, axis=1, keepdims=True)
    normed = (stream * lax.rsqrt(mean_square + 1e-05) * norm_gain).astype(jnp.bfloat16)
    stream = lax.dynamic_slice_in_dim(stream, offset, half_cols, 1)
    normed = lax.dynamic_slice_in_dim(normed, offset, half_cols, 1)
    return routed_slots(
        stream, normed, experts_chosen, router_logits, w_gate, w_up, w_down, capacity
    )


def solution(mesh):
    return jax.shard_map(
        layer,
        mesh=mesh,
        in_specs=(
            P(("rep", "ep"), None),
            P(("rep", "ep"), "tp"),
            P(None, ("rep", "ep"), None, "tp"),
            P(("rep", "ep"), None),
            P(("rep", "ep")),
            P(("rep", "ep"), None),
            P(("rep", "ep"), None),
            P(),
            P("tp", None),
            P("ep", None, "tp"),
            P("ep", None, "tp"),
            P("ep", "tp", None),
        ),
        out_specs=P(("rep", "ep"), "tp"),
        check_vma=False,
    )
```

```python
import functools
import math

import jax
import jax.numpy as jnp
from jax import lax
from jax.experimental import pallas as pl
from jax.experimental.pallas import tpu as pltpu
from jax.sharding import PartitionSpec as P


HEAD_WIDTH = 64
LANES = 128
MIB = 1 << 20
ATTEND_MIB = 36

SMEM = pl.BlockSpec(memory_space=pltpu.SMEM)
VMEM = pl.BlockSpec(memory_space=pltpu.VMEM)
HBM = pl.BlockSpec(memory_space=pltpu.HBM)


def dense_gates(experts, chosen, logits, out):
    tokens, columns = out.shape
    gate = jnp.exp(logits[...] - jnp.max(logits[...], axis=0, keepdims=True))
    gate = gate / jnp.sum(gate, axis=0, keepdims=True)
    name = lax.broadcasted_iota(jnp.int32, (columns, tokens), 0)
    fine = name >= experts
    expert = jnp.where(fine, name - experts, name)
    dense = jnp.zeros((columns, tokens), jnp.float32)
    for k in range(chosen.shape[0]):
        dense += jnp.where(chosen[k : k + 1, :] == expert, gate[k : k + 1, :], 0.0)
    coarse = dense.astype(jnp.bfloat16).astype(jnp.float32)
    both = jnp.where(fine, dense - coarse, coarse).astype(jnp.bfloat16)
    row = lax.broadcasted_iota(jnp.int32, (columns, columns), 0)
    unit = (row == lax.broadcasted_iota(jnp.int32, (columns, columns), 1)).astype(jnp.bfloat16)
    turned = lax.dot_general(both, unit, (((0,), (0,)), ((), ())), preferred_element_type=jnp.float32)
    out[...] = turned.astype(jnp.bfloat16)


def attend_kernel(
    heads,
    experts,
    table_in,
    length_in,
    q_in,
    pages,
    proj,
    chosen_in,
    logits_in,
    *refs,
):
    count = (len(refs) - 15) // 2
    weights_in, (out_wide, out_sent, out_gates) = refs[:count], refs[count : count + 3]
    weights_out, refs = refs[count + 3 : 2 * count + 3], refs[2 * count + 3 :]
    table, length, q, chosen, logits, kbuf, vbuf, wbuf, qs, ws, os, sem = refs
    tokens = q.shape[0]
    per_token = table.shape[0]
    lanes = kbuf.shape[2]
    positions = per_token * kbuf.shape[1]
    moves = (
        (q_in, q),
        (chosen_in, chosen),
        (logits_in, logits),
        (table_in, table),
        (length_in, length),
        (pages.at[0], kbuf),
        (pages.at[1], vbuf),
        (proj, wbuf),
        *zip(weights_in, weights_out),
    )
    copies = [pltpu.make_async_copy(*move, sem.at[i]) for i, move in enumerate(moves)]
    small, (keys_in, values_in, proj_in), experts_in = copies[:5], copies[5:8], copies[8:]
    for copy in copies:
        copy.start()
    small[0].wait()
    low = lax.broadcasted_iota(jnp.int32, (tokens, lanes), 1) < HEAD_WIDTH
    half = heads // 2
    for h in range(heads):
        pair = q[:, (h // 2) * lanes : (h // 2 + 1) * lanes].astype(jnp.float32)
        if (h < half) != (h % 2 == 0):
            pair = pltpu.roll(pair, HEAD_WIDTH, 1)
        row = jnp.where(low if h < half else ~low, pair, 0.0)
        qs[pl.ds(h, tokens, stride=heads), :] = row * (1.0 / math.sqrt(HEAD_WIDTH))
    for copy in small[1:]:
        copy.wait()
    dense_gates(experts, chosen, logits, out_gates)
    keys_in.wait()
    spot = lax.broadcasted_iota(jnp.int32, (heads, positions), 1)

    def tiles(buffer, t):
        return jnp.concatenate([buffer[table[i, t]] for i in range(per_token)], axis=0)

    scores = []
    for t in range(tokens):
        rows = qs[t * heads : (t + 1) * heads, :].astype(jnp.bfloat16)
        s = lax.dot_general(
            rows, tiles(kbuf, t), (((1,), (1,)), ((), ())), preferred_element_type=jnp.float32
        )
        scores.append(jnp.where(spot < length[t], s, -jnp.inf))
    s = jnp.concatenate(scores, axis=0)
    w = jnp.exp(s - jnp.max(s, axis=1, keepdims=True))
    ws[...] = (w / jnp.sum(w, axis=1, keepdims=True)).astype(jnp.bfloat16)
    values_in.wait()
    for t in range(tokens):
        rows = slice(t * heads, (t + 1) * heads)
        os[rows, :] = jnp.dot(ws[rows, :], tiles(vbuf, t), preferred_element_type=jnp.float32)

    parts = []
    for j in range(half):
        even = os[pl.ds(2 * j, tokens, stride=heads), :]
        odd = os[pl.ds(2 * j + 1, tokens, stride=heads), :]
        if 2 * j < half:
            odd = pltpu.roll(odd, HEAD_WIDTH, 1)
        else:
            even = pltpu.roll(even, HEAD_WIDTH, 1)
        parts.append(jnp.where(low, even, odd).astype(jnp.bfloat16))
    attended = jnp.concatenate(parts, axis=1)
    proj_in.wait()
    part = lax.dot_general(
        attended, wbuf[...], (((1,), (1,)), ((), ())), preferred_element_type=jnp.float32
    )
    out_wide[...] = part
    out_sent[...] = part.astype(jnp.bfloat16)
    for copy in experts_in:
        copy.wait()


def attend(query, pages, page_table, ctx_len, out_proj, chosen, logits, experts, weights):
    tokens = query.shape[0]
    heads = query.shape[1] // HEAD_WIDTH
    width = out_proj.shape[1]
    lanes = pages.shape[3]
    rows = (tokens * heads, lanes)
    operands = (page_table.T, ctx_len, query, pages, out_proj.T, chosen.T, logits.T, *weights)
    operands = [pltpu.with_memory_space_constraint(v, pltpu.HBM) for v in operands]
    return pl.pallas_call(
        functools.partial(attend_kernel, heads, experts),
        out_shape=(
            jax.ShapeDtypeStruct((tokens, width), jnp.float32),
            jax.ShapeDtypeStruct((tokens, width), jnp.bfloat16),
            jax.ShapeDtypeStruct((tokens, 2 * experts), jnp.bfloat16),
            *[jax.ShapeDtypeStruct(w.shape, w.dtype) for w in weights],
        ),
        in_specs=[HBM] * len(operands),
        out_specs=(VMEM,) * (3 + len(weights)),
        scratch_shapes=[
            pltpu.SMEM(operands[0].shape, jnp.int32),
            pltpu.SMEM(operands[1].shape, jnp.int32),
            pltpu.VMEM(query.shape, query.dtype),
            pltpu.VMEM(operands[5].shape, jnp.int32),
            pltpu.VMEM(operands[6].shape, jnp.float32),
            pltpu.VMEM(pages.shape[1:], pages.dtype),
            pltpu.VMEM(pages.shape[1:], pages.dtype),
            pltpu.VMEM(operands[4].shape, out_proj.dtype),
            pltpu.VMEM(rows, jnp.float32),
            pltpu.VMEM((rows[0], page_table.shape[1] * pages.shape[2]), jnp.bfloat16),
            pltpu.VMEM(rows, jnp.float32),
            pltpu.SemaphoreType.DMA((8 + len(weights),)),
        ],
        compiler_params=pltpu.CompilerParams(vmem_limit_bytes=ATTEND_MIB * MIB),
        name="attend",
    )(*operands)


def norm_kernel(resid, own, other, gain, gates, stream_out, all_out, mine_out):
    tokens, width = own.shape
    side = lax.axis_index("tp")
    half_cols = stream_out.shape[1]
    stream = resid[...].astype(jnp.float32) + own[...] + other[...].astype(jnp.float32)
    mean_square = jnp.sum(stream * stream, axis=1, keepdims=True) / width
    normed = stream * lax.rsqrt(mean_square + 1e-05) * gain[...]
    all_out[:, :width] = normed.astype(jnp.bfloat16)
    all_out[:, width : width + gates.shape[1]] = gates[...]
    rows = tokens // 2
    mine_out[...] = all_out[pl.ds(pl.multiple_of(side * rows, rows), rows), :]
    stream_out[...] = jnp.where(side == 0, stream[:, :half_cols], stream[:, half_cols:])


def norm(resid, own, other, gain, gates, padded):
    tokens, width = own.shape
    return pl.pallas_call(
        norm_kernel,
        out_shape=(
            jax.ShapeDtypeStruct((tokens, width // 2), jnp.float32),
            jax.ShapeDtypeStruct((tokens, padded), jnp.bfloat16),
            jax.ShapeDtypeStruct((tokens // 2, padded), jnp.bfloat16),
        ),
        in_specs=[VMEM] * 5,
        out_specs=(VMEM,) * 3,
        compiler_params=pltpu.CompilerParams(vmem_limit_bytes=4 * MIB),
        name="norm",
    )(resid, own, other, gain[None], gates)


def expert_kernel(experts, pieces, *refs):
    sources = refs[:pieces]
    w_gate, w_up, w_down, keep_out, send_out, xs = refs[pieces:]
    side = lax.axis_index("tp")
    me = lax.axis_index("ep")
    width = w_gate.shape[0]
    if pieces == 1:
        xs = sources[0]
    else:
        rows = sources[0].shape[0]
        for b in range(pieces // 2):
            here = pl.multiple_of(b * 2 * rows + side * rows, rows)
            there = pl.multiple_of(b * 2 * rows + (1 - side) * rows, rows)
            xs[pl.ds(here, rows), :] = sources[2 * b][...]
            xs[pl.ds(there, rows), :] = sources[2 * b + 1][...]
    x = xs[:, :width]
    spare = xs[:, width : width + 2 * experts].astype(jnp.float32)
    column = lax.broadcasted_iota(jnp.int32, spare.shape, 1)
    mine = (column == me) | (column == me + experts)
    gate = jnp.sum(jnp.where(mine, spare, 0.0), axis=1, keepdims=True)
    g = jnp.dot(x, w_gate[...], preferred_element_type=jnp.float32)
    u = jnp.dot(x, w_up[...], preferred_element_type=jnp.float32)
    hidden = (g * jax.nn.sigmoid(1.702 * g) * (u + 1.0)).astype(jnp.bfloat16)
    y = jnp.dot(hidden, w_down[...], preferred_element_type=jnp.float32) * gate
    half_cols = y.shape[1] // 2
    left, right = y[:, :half_cols], y[:, half_cols:]
    keep_out[:, :half_cols] = jnp.where(side == 0, left, right)
    send_out[:, :half_cols] = jnp.where(side == 0, right, left).astype(jnp.bfloat16)


def expert(sources, w_gate, w_up, w_down, experts):
    pieces = len(sources)
    rows = sum(s.shape[0] for s in sources)
    padded = sources[0].shape[1]
    out_cols = -(-w_down.shape[1] // 2 // LANES) * LANES
    return pl.pallas_call(
        functools.partial(expert_kernel, experts, pieces),
        out_shape=(
            jax.ShapeDtypeStruct((rows, out_cols), jnp.float32),
            jax.ShapeDtypeStruct((rows, out_cols), jnp.bfloat16),
        ),
        in_specs=[VMEM] * (pieces + 3),
        out_specs=(VMEM,) * 2,
        scratch_shapes=[pltpu.VMEM((rows if pieces > 1 else 16, padded), jnp.bfloat16)],
        compiler_params=pltpu.CompilerParams(vmem_limit_bytes=16 * MIB),
        cost_estimate=pl.CostEstimate(
            flops=6 * rows * w_down.size, transcendentals=0, bytes_accessed=6 * w_down.size
        ),
        name="expert",
    )(*sources, w_gate, w_up, w_down)


def flip(value, axis, offset):
    return lax.ppermute(value, axis, [(i, i ^ offset) for i in range(lax.axis_size(axis))])


GROUPS = (('own', (0,)), ('near', (1, 2, 4)), ('far', (5, 6)), ('last', (3, 7)))
APART = ('own', 'near')
ROWS = {4: 0, 2: 0, 1: 0, 7: 0, 6: 4, 5: 4, 3: 2}
BACK = {7: 0, 6: 4, 5: 4, 3: 2, 4: 0, 2: 0, 1: 0}


def routed_all(stream, whole, mine, weights, experts):
    tokens = whole.shape[0]
    cols = stream.shape[1]
    half = {0: mine}
    for k, source in ROWS.items():
        half[k] = flip(half[source], "ep", k ^ source)
    total = {}
    for name, group in GROUPS:
        sources = [whole]
        if name != "own":
            sources = []
            for k in group:
                sources += [half[k], flip(half[k], "tp", 1)]
        kept, sent = expert(sources, *weights, experts)
        received = flip(sent, "tp", 1)
        sums = []
        for i, k in enumerate(group):
            rows = slice(i * tokens, (i + 1) * tokens)
            sums.append(kept[rows] + received[rows].astype(jnp.float32))
        if name in APART:
            sums = lax.optimization_barrier(tuple(sums))
        total.update(zip(group, sums))
    for k, target in BACK.items():
        part = flip(total[k].astype(jnp.bfloat16), "ep", k ^ target)
        total[target] = total[target] + part.astype(jnp.float32)
    return (stream + total[0][:, :cols]).astype(jnp.bfloat16)


def routed_slots(stream, normed, experts_chosen, router_logits, w_gate, w_up, w_down, capacity):
    tok_rows, top_count = experts_chosen.shape
    local_experts = w_gate.shape[0]
    owners = lax.axis_size("ep")
    experts = local_experts * owners
    gate_weights = jax.nn.softmax(router_logits, axis=1)
    chosen_flat = experts_chosen.reshape(-1)
    onehot = (chosen_flat[:, None] == jnp.arange(experts, dtype=jnp.int32)[None, :]).astype(
        jnp.int32
    )
    before = jnp.cumsum(onehot, axis=0, dtype=jnp.int32) - onehot
    slot_rank = jnp.sum(before * onehot, axis=1, dtype=jnp.int32)
    slot_index = (chosen_flat * capacity + slot_rank).reshape(tok_rows, top_count)
    slot_range = jnp.arange(experts * capacity, dtype=jnp.int32)
    placed = slot_index[:, :, None] == slot_range[None, None, :]
    dispatch = jnp.sum(placed.astype(jnp.float32), axis=1).astype(jnp.bfloat16)
    outgoing = lax.dot_general(
        dispatch, normed, (((0,), (0,)), ((), ())), preferred_element_type=jnp.float32
    )
    outgoing = outgoing.astype(jnp.bfloat16).reshape(
        owners, local_experts, capacity, normed.shape[1]
    )
    arrived_full = lax.all_gather(
        lax.all_to_all(outgoing, "ep", split_axis=0, concat_axis=0, tiled=True),
        "tp",
        axis=3,
        tiled=True,
    )
    gate_value = jnp.einsum(
        "sekd,edf->sekf", arrived_full, w_gate, preferred_element_type=jnp.float32
    )
    up_value = jnp.einsum("sekd,edf->sekf", arrived_full, w_up, preferred_element_type=jnp.float32)
    hidden = (gate_value * jax.nn.sigmoid(1.702 * gate_value) * (up_value + 1.0)).astype(
        jnp.bfloat16
    )
    partial_value = jnp.einsum("sekf,efd->sekd", hidden, w_down, preferred_element_type=jnp.float32)
    finished = lax.psum_scatter(partial_value, "tp", scatter_dimension=3, tiled=True).astype(
        jnp.bfloat16
    )
    returned = lax.all_to_all(finished, "ep", split_axis=0, concat_axis=0, tiled=True)
    combine = jnp.sum(placed.astype(jnp.float32) * gate_weights[:, :, None], axis=1)
    expert_mix = jnp.dot(
        combine,
        returned.reshape(experts * capacity, -1).astype(jnp.float32),
        precision=lax.Precision.HIGHEST,
    )
    return (stream + expert_mix).astype(jnp.bfloat16)


def layer(
    resid,
    query,
    key_value_pages,
    page_table,
    ctx_len,
    experts_chosen,
    router_logits,
    norm_gain,
    out_proj,
    w_gate,
    w_up,
    w_down,
):
    tok_rows, model_width = resid.shape
    top_count = experts_chosen.shape[1]
    local_experts = w_gate.shape[0]
    owners = lax.axis_size("ep")
    experts = local_experts * owners
    capacity = max(2, min(tok_rows, 2 * tok_rows * top_count // experts))
    padded = -(-model_width // LANES) * LANES

    dense = (
        local_experts == 1
        and tok_rows <= capacity
        and model_width + 2 * experts <= padded
        and owners & (owners - 1) == 0
    )
    own, sent, gates, *weights = attend(
        query,
        key_value_pages,
        page_table,
        ctx_len,
        out_proj,
        experts_chosen,
        router_logits,
        experts,
        (w_gate[0], w_up[0], w_down[0]) if dense else (),
    )
    other = flip(sent, "tp", 1)
    if dense:
        stream, whole, mine = norm(resid, own, other, norm_gain, gates, padded)
        return routed_all(stream, whole, mine, weights, experts)
    half_cols = model_width // lax.axis_size("tp")
    offset = lax.axis_index("tp") * half_cols
    stream = resid.astype(jnp.float32) + own + other.astype(jnp.float32)
    mean_square = jnp.mean(stream * stream, axis=1, keepdims=True)
    normed = (stream * lax.rsqrt(mean_square + 1e-05) * norm_gain).astype(jnp.bfloat16)
    stream = lax.dynamic_slice_in_dim(stream, offset, half_cols, 1)
    normed = lax.dynamic_slice_in_dim(normed, offset, half_cols, 1)
    return routed_slots(
        stream, normed, experts_chosen, router_logits, w_gate, w_up, w_down, capacity
    )


def solution(mesh):
    return jax.shard_map(
        layer,
        mesh=mesh,
        in_specs=(
            P(("rep", "ep"), None),
            P(("rep", "ep"), "tp"),
            P(None, ("rep", "ep"), None, "tp"),
            P(("rep", "ep"), None),
            P(("rep", "ep")),
            P(("rep", "ep"), None),
            P(("rep", "ep"), None),
            P(),
            P("tp", None),
            P("ep", None, "tp"),
            P("ep", None, "tp"),
            P("ep", "tp", None),
        ),
        out_specs=P(("rep", "ep"), "tp"),
        check_vma=False,
    )
```
